512 devices in a mesh: tok: 32 (over y, x, core), voc: 16 (over z).
Axes of the slice: x: 4, y: 4, z: 16, core: 2. Of those that a mesh axis runs over, the one named last changes fastest.
Arguments:
- student_hidden: bfloat16 [512, 2560], P('tok', 'voc'), may hold values from -72 to 72
- teacher_rows: bfloat16 [512, 4096], P('tok', 'voc'), may hold values from -72 to 72
- student_head: bfloat16 [2560, 131072], P(None, ('tok', 'voc')), may hold values from -0.375 to 0.375
- teacher_head: bfloat16 [4096, 131072], P(None, ('tok', 'voc')), may hold values from -0.25 to 0.25
- lengths: int32 [32], replicated, may hold values from 1 to 16, 320 in all
- route: int32 [512], replicated, may hold values from 0 to 511, each once
- sampled_ids: int32 [512], replicated, may hold values from 0 to 131071
- mix_flags: int32 [512], replicated, may hold values 0 or 1
Outputs:
- divergence: float32 [512], P('tok')
- head_grad: bfloat16 [2560, 131072], P(None, ('tok', 'voc'))
The draws below stay inside these ranges and needn't reach their ends.
Inputs may be any that keep to these rules, and one draw needn't show every extreme that they name: The lengths sum to 320; the largest is exactly 16. `route`: each trainer position appears once.
All inputs are finite; a program needn't handle non-finite values.
Results may differ from the reference program's by a relative error of at most 0.0052.
Values may be sent and summed in bfloat16 or wider, within the bound.
No kernel may reach another device: no remote copies, remote signals or barrier semaphores. Data moves between devices by JAX's collectives and lax.ppermute only.
A program may use at most 64 MiB of HBM per device.

```python
import math
import jax
import jax.numpy as jnp
import numpy as np
from jax import lax

DS = 2560
DT = 4096
TOK_GRP = 16
TOKENS = 512
LIVE = 320
V = 131072
N_TOK = 32


def hidden_rows(key, width, shown_scale):
    values = jnp.clip(jax.random.normal(key, (TOKENS, width), jnp.float32), -6.0, 6.0)
    values = values * shown_scale
    return values.astype(jnp.bfloat16)


def draw_student_hidden(key, part):
    return hidden_rows(jax.random.fold_in(key, 11), DS, 0.5)


def draw_teacher_rows(key, part):
    return hidden_rows(jax.random.fold_in(key, 23), DT, 1.0)


def set_ends(array, rng, least, high):
    shape = array.shape
    place = [jax.random.randint(jax.random.fold_in(rng, axis), (), 0, shape[axis]) for axis in range(len(shape))]
    array = array.at[tuple(place)].set(least)
    longest = shape.index(max(shape))
    place[longest] = (place[longest] + 1) % shape[longest]
    return array.at[tuple(place)].set(high)


def level_of(rng, extent, pieces, least, high):
    def one(dim, parts):
        heights = jax.random.uniform(jax.random.fold_in(jax.random.fold_in(rng, 6), dim), (parts,), jnp.float32, least / len(pieces), high / len(pieces))
        return jnp.repeat(jnp.exp(heights), extent[dim] // parts).reshape((-1,) + (1,) * (len(extent) - dim - 1))

    factor_of = one(*pieces[0])
    for cut in pieces[1:]:
        factor_of = factor_of * one(*cut)
    return factor_of


def profile(count, total, most, slope):
    portions = [(1 << 20) // math.isqrt(grade ** slope) + 1 for grade in range(2, count + 1)]
    spare, counts = total - most - (count - 1), [1] * (count - 1)
    while spare > 0:
        candidates = [i for i in range(count - 1) if counts[i] < most]
        mass, remaining = sum([portions[i] for i in candidates]), spare
        for i in candidates:
            extra = min(most - counts[i], max(1, remaining * portions[i] // mass), spare)
            counts[i] = counts[i] + extra
            spare = spare - extra
    return np.array([most] + counts)


def uneven(stream_key, amount, total, reach, slope):
    if amount == 2:
        one = jax.random.randint(stream_key, (), max(1, total - reach), min(reach, total - 1) + 1)
        return jnp.stack([one, total - one])
    sizes = jnp.asarray(profile(amount, total, reach, slope), jnp.int32)
    couples = (amount - 1) // 2
    source_of, taker = sizes[1:1 + 2 * couples:2], sizes[2:2 + 2 * couples:2]
    slack = jnp.minimum(source_of - 1, reach - taker)
    moved = jax.random.randint(jax.random.fold_in(stream_key, 1), (couples,), 0, 1 << 20) % (slack + 1)
    sizes = sizes.at[1:1 + 2 * couples:2].set(source_of - moved).at[2:2 + 2 * couples:2].set(taker + moved)
    return sizes[jax.random.permutation(jax.random.fold_in(stream_key, 2), amount)]


def gaussian(stream_key, dims, spread, limit, split=(), kind=jnp.bfloat16):
    array = spread * jax.random.normal(stream_key, dims, jnp.float32)
    if split:
        array = array * level_of(stream_key, dims, split, -0.22, 0.18)
    return jnp.clip(array, -limit, limit).astype(kind)


def setup_inputs(seed: int = 0) -> dict:
    streams_of = jax.random.split(jax.random.key(seed), 9)
    student_hidden = draw_student_hidden(jax.random.fold_in(streams_of[8], 71), 0)
    teacher_rows = draw_teacher_rows(jax.random.fold_in(streams_of[8], 71), 0)
    student_head = gaussian(streams_of[2], (DS, V), (DS // 9) ** -0.5, 0.375, ((1, 512),))
    teacher_head = gaussian(streams_of[3], (DT, V), (DT // 9) ** -0.5, 0.25, ((1, 512),))
    lengths = uneven(streams_of[4], N_TOK, LIVE, TOK_GRP, 2).astype(jnp.int32)
    route = jax.random.permutation(streams_of[5], TOKENS).astype(jnp.int32)
    sampled_ids = set_ends(jax.random.randint(streams_of[6], (TOKENS,), 0, V), jax.random.fold_in(streams_of[6], 1), 0, V - 1).astype(jnp.int32)
    mix_flags = set_ends((jax.random.randint(streams_of[7], (TOKENS,), 0, 2) < 1).astype(jnp.int32), jax.random.fold_in(streams_of[7], 1), 0, 1)
    return dict(student_hidden=student_hidden, teacher_rows=teacher_rows, student_head=student_head, teacher_head=teacher_head, lengths=lengths, route=route, sampled_ids=sampled_ids, mix_flags=mix_flags)


def reference(student_hidden, teacher_rows, student_head, teacher_head, lengths, route, sampled_ids, mix_flags):
    position = jnp.arange(TOKENS, dtype=jnp.int32)
    live = ((position % TOK_GRP) < lengths[position // TOK_GRP]).astype(jnp.float32)
    teacher_hidden = jnp.zeros_like(teacher_rows).at[route].set(teacher_rows)
    student_logits = jnp.dot(student_hidden, student_head, preferred_element_type=jnp.float32)
    teacher_logits = jnp.dot(teacher_hidden, teacher_head, preferred_element_type=jnp.float32)
    log_student = jax.nn.log_softmax(student_logits, axis=-1)
    log_teacher = jax.nn.log_softmax(teacher_logits, axis=-1)
    probs = jnp.exp(log_student)
    gap = log_student - log_teacher
    kl_all = jnp.sum(probs * gap, axis=-1)
    student_pick = jnp.take_along_axis(log_student, sampled_ids[:, None], axis=1)[:, 0]
    teacher_pick = jnp.take_along_axis(log_teacher, sampled_ids[:, None], axis=1)[:, 0]
    mixed = 1.0 / (0.2 * jnp.exp(teacher_pick - student_pick) + 0.8)
    weight = jnp.where(mix_flags == 1, mixed, jnp.ones_like(mixed))
    divergence = live * kl_all
    dlogits = ((live * weight)[:, None] * probs * (gap - kl_all[:, None])).astype(jnp.bfloat16)
    head_grad = lax.dot_general(student_hidden, dlogits, (((0,), (0,)), ((), ())), preferred_element_type=jnp.float32)
    return divergence, head_grad.astype(jnp.bfloat16)
```

```python
import jax
import jax.numpy as jnp
from jax import lax
from jax.experimental import pallas as pl
from jax.experimental.pallas import tpu as pltpu
from jax.sharding import Mesh, PartitionSpec as P

F32 = jnp.float32
BF16 = jnp.bfloat16
VMEM = pl.BlockSpec(memory_space=pltpu.VMEM)
SMEM = pl.BlockSpec(memory_space=pltpu.SMEM)
LIMIT = pltpu.CompilerParams(vmem_limit_bytes=56 * 1024 * 1024)


def spread_kernel(gathered, out):
    nz = gathered.shape[0]
    teacher = [gathered[z, :, :256] for z in range(nz)]
    student = [gathered[z, :, 256:] for z in range(nz)]
    whole = jnp.concatenate(teacher + student, axis=1)
    for i in range(out.shape[0]):
        out[i] = whole


def half_kernel(rows, head_s, head_t, s_out, u_out):
    dt = head_t.shape[0]
    s_out[...] = jnp.dot(rows[:, dt:], head_s[...], preferred_element_type=F32)
    u_out[...] = jnp.dot(rows[:, :dt], head_t[...], preferred_element_type=F32)


def store_stats(out, values):
    for k, value in enumerate(values):
        tiles = value.shape[1] // 128
        for j in range(tiles):
            out[k * tiles + j : k * tiles + j + 1, :] = value[:, 128 * j : 128 * j + 128]


def stats_kernel(
    where, rows, head_s, head_t, s_own, u_own, route, ids, s_t_out, u_t_out, stats_out, s_nat, u_nat
):
    core, first_col = where[0], where[1]
    dt = head_t.shape[0]
    tokens = s_nat.shape[0]
    halves = (
        (core, s_own[...], u_own[...]),
        (
            1 - core,
            jnp.dot(rows[:, dt:], head_s[...], preferred_element_type=F32),
            jnp.dot(rows[:, :dt], head_t[...], preferred_element_type=F32),
        ),
    )
    for half, s_half, u_half in halves:
        for j in range(tokens // 32):
            at = pl.ds(pl.multiple_of((2 * j + half) * 16, 16), 16)
            s_nat[at, :] = s_half[16 * j : 16 * j + 16]
            u_nat[at, :] = u_half[16 * j : 16 * j + 16]
    s_t = s_nat[...].T
    u_roll = u_nat[...].T
    order = lax.broadcasted_iota(jnp.int32, (tokens, tokens), 0)
    pick = jnp.where(order == route[...], 1.0, 0.0).astype(BF16)
    high = u_roll.astype(BF16)
    rest = u_roll - high.astype(F32)
    middle = rest.astype(BF16)
    low = (rest - middle.astype(F32)).astype(BF16)
    u_t = jnp.zeros_like(u_roll)
    for part in (low, middle, high):
        u_t = u_t + lax.dot_general(
            part, pick, (((1,), (1,)), ((), ())), preferred_element_type=F32
        )
    s_t_out[...] = s_t
    u_t_out[...] = u_t
    m_s = jnp.max(s_t, axis=0, keepdims=True)
    m_u = jnp.max(u_t, axis=0, keepdims=True)
    s_rel = s_t - m_s
    u_rel = u_t - m_u
    e_s = jnp.exp(s_rel)
    sum_s = jnp.sum(e_s, axis=0, keepdims=True)
    sum_u = jnp.sum(jnp.exp(u_rel), axis=0, keepdims=True)
    mean = jnp.sum(e_s * (s_rel - u_rel), axis=0, keepdims=True) / sum_s
    log_s = jnp.log(sum_s)
    log_u = jnp.log(sum_u)
    column = lax.broadcasted_iota(jnp.int32, s_t.shape, 0)
    hit = column == ids[...] - first_col
    apart = jnp.sum(jnp.where(hit, u_t - s_t, 0.0), axis=0, keepdims=True)
    store_stats(stats_out, (m_s + log_s, m_u + log_u, mean - log_s + log_u, apart))


def merge(parts):
    lse_s, lse_u = parts[:, 0:4], parts[:, 4:8]
    kl, apart = parts[:, 8:12], parts[:, 12:16]
    m_s = jnp.max(lse_s, axis=0)
    m_u = jnp.max(lse_u, axis=0)
    all_s = m_s + jnp.log(jnp.sum(jnp.exp(lse_s - m_s), axis=0))
    all_u = m_u + jnp.log(jnp.sum(jnp.exp(lse_u - m_u), axis=0))
    share = jnp.exp(lse_s - all_s)
    whole = jnp.sum(share * (kl + (lse_s - all_s) - (lse_u - all_u)), axis=0)
    return all_s, all_u, whole, jnp.sum(apart, axis=0)


def merge_kernel(parts, out):
    merged = jnp.concatenate(merge(parts[...]), axis=0)
    for i in range(out.shape[0]):
        out[i] = merged


def grad_kernel(
    where, lengths, parts, s_t, u_t, flags, own, other, kl_out, grad_out, dl_nat, dl_half
):
    core = where[0]
    tokens = dl_nat.shape[0]
    dt = own.shape[1] - grad_out.shape[0]

    def lanes(rows):
        return jnp.concatenate([rows[j : j + 1] for j in range(4)], axis=1)

    lse_s, lse_u, kl, apart = [lanes(v) for v in merge(parts[...])]
    slot = lax.broadcasted_iota(jnp.int32, (1, tokens), 1)
    length = jnp.zeros((1, tokens), jnp.int32)
    for w in range(lengths.shape[0]):
        length = jnp.where(slot // 16 == w, lengths[w], length)
    live = (slot % 16 < length).astype(F32)
    mixed = 1.0 / (0.2 * jnp.exp(apart - lse_u + lse_s) + 0.8)
    weight = jnp.where(flags[...] == 1, mixed, jnp.ones_like(mixed))
    kl_out[...] = live * kl
    log_s = s_t[...] - lse_s
    gap = log_s - (u_t[...] - lse_u)
    d_t = (live * weight) * jnp.exp(log_s) * (gap - kl)
    dl_nat[...] = d_t.T
    for n, half in enumerate((core, 1 - core)):
        for j in range(tokens // 32):
            at = pl.ds(pl.multiple_of((2 * j + half) * 16, 16), 16)
            dl_half[n, 16 * j : 16 * j + 16, :] = dl_nat[at, :].astype(BF16)
    step = 512
    for f in range(0, grad_out.shape[0], step):
        total = jnp.zeros((grad_out.shape[1], step), F32)
        for n, rows in enumerate((own, other)):
            total = total + lax.dot_general(
                dl_half[n], rows[:, dt + f : dt + f + step], (((0,), (0,)), ((), ())),
                preferred_element_type=F32,
            )
        grad_out[f : f + step, :] = total.T.astype(BF16)


def on_device(
    student_hidden, teacher_rows, student_head, teacher_head, lengths, route, sampled_ids, mix_flags
):
    ny, nx, nz = lax.axis_size("y"), lax.axis_size("x"), lax.axis_size("z")
    core = lax.axis_index("c")
    group = (lax.axis_index("y") * nx + lax.axis_index("x")) * 2 + core
    grp_rows = student_hidden.shape[0]
    ds, vocab_dev = student_head.shape
    dt = teacher_head.shape[0]
    tokens = route.shape[0]
    half = tokens // 2
    first_col = (group * nz + lax.axis_index("z")) * vocab_dev
    where = jnp.stack([core, first_col]).astype(jnp.int32)

    local = jnp.concatenate([teacher_rows, student_hidden], axis=1)
    gathered = lax.all_to_all(jnp.broadcast_to(local, (nz,) + local.shape), "z", 0, 0)
    copies = pl.pallas_call(
        spread_kernel,
        out_shape=jax.ShapeDtypeStruct((ny * nx, grp_rows, dt + ds), BF16),
        in_specs=[VMEM], out_specs=VMEM, compiler_params=LIMIT,
    )(gathered)
    own = lax.all_to_all(copies, ("y", "x"), 0, 0).reshape(half, dt + ds)
    other = lax.ppermute(own, "c", [(0, 1), (1, 0)])
    logits = jax.ShapeDtypeStruct((half, vocab_dev), F32)
    s_own, u_own = pl.pallas_call(
        half_kernel, out_shape=(logits, logits),
        in_specs=[VMEM] * 3, out_specs=(VMEM, VMEM), compiler_params=LIMIT,
    )(own, student_head, teacher_head)
    whole = jax.ShapeDtypeStruct((vocab_dev, tokens), F32)
    s_t, u_t, stats = pl.pallas_call(
        stats_kernel,
        out_shape=(whole, whole, jax.ShapeDtypeStruct((4 * tokens // 128, 128), F32)),
        in_specs=[SMEM] + [VMEM] * 7, out_specs=(VMEM,) * 3,
        scratch_shapes=[pltpu.VMEM((tokens, vocab_dev), F32)] * 2, compiler_params=LIMIT,
    )(where, other, student_head, teacher_head, s_own, u_own, route[None], sampled_ids[None])
    near = lax.all_to_all(jnp.broadcast_to(stats, (2 * ny * nx,) + stats.shape), ("y", "x", "c"), 0, 0)
    merged = pl.pallas_call(
        merge_kernel,
        out_shape=jax.ShapeDtypeStruct((nz,) + stats.shape, F32),
        in_specs=[VMEM], out_specs=VMEM,
    )(near)
    far = lax.all_to_all(merged, "z", 0, 0)
    kl_rows, head_grad = pl.pallas_call(
        grad_kernel,
        out_shape=(
            jax.ShapeDtypeStruct((1, tokens), F32),
            jax.ShapeDtypeStruct((ds, vocab_dev), BF16),
        ),
        in_specs=[SMEM] * 2 + [VMEM] * 6, out_specs=(VMEM,) * 2,
        scratch_shapes=[
            pltpu.VMEM((tokens, vocab_dev), F32), pltpu.VMEM((2, half, vocab_dev), BF16)
        ],
        compiler_params=LIMIT,
    )(where, lengths, far, s_t, u_t, mix_flags[None], own, other)
    divergence = lax.dynamic_slice_in_dim(kl_rows[0], group * grp_rows, grp_rows)
    return divergence, head_grad


def solution(mesh):
    fine = Mesh(mesh.devices.reshape(4, 4, 2, 16), ("y", "x", "c", "z"))
    tok = ("y", "x", "c")
    every = tok + ("z",)
    in_specs = (P(tok, "z"), P(tok, "z"), P(None, every), P(None, every), P(), P(), P(), P())
    out_specs = (P(tok), P(None, every))
    return jax.shard_map(
        on_device, mesh=fine, in_specs=in_specs, out_specs=out_specs, check_vma=False
    )
```

```python
import jax
import jax.numpy as jnp
from jax import lax
from jax.experimental import pallas as pl
from jax.experimental.pallas import tpu as pltpu
from jax.sharding import Mesh, PartitionSpec as P

F32 = jnp.float32
BF16 = jnp.bfloat16
VMEM = pl.BlockSpec(memory_space=pltpu.VMEM)
SMEM = pl.BlockSpec(memory_space=pltpu.SMEM)


def grant(mib):
    return pltpu.CompilerParams(vmem_limit_bytes=mib * 1024 * 1024)


def spread_kernel(gathered, out):
    nz = gathered.shape[0]
    teacher = [gathered[z, :, :256] for z in range(nz)]
    student = [gathered[z, :, 256:] for z in range(nz)]
    whole = jnp.concatenate(teacher + student, axis=1)
    for i in range(out.shape[0]):
        out[i] = whole


def half_kernel(rows, head_s, head_t, s_out, u_out):
    dt = head_t.shape[0]
    s_out[...] = jnp.dot(rows[:, dt:], head_s[...], preferred_element_type=F32)
    u_out[...] = jnp.dot(rows[:, :dt], head_t[...], preferred_element_type=F32)


def store_stats(out, values):
    rows = [v[:, 128 * j : 128 * j + 128] for v in values for j in range(v.shape[1] // 128)]
    block = jnp.concatenate(rows, axis=0)
    for i in range(out.shape[0]):
        out[i] = block


def stats_kernel(
    where, rows, head_s, head_t, s_own, u_own, route, ids, s_t_out, u_t_out, stats_out, s_nat, u_nat
):
    core, first_col = where[0], where[1]
    dt = head_t.shape[0]
    tokens = s_nat.shape[0]
    halves = (
        (core, s_own[...], u_own[...]),
        (
            1 - core,
            jnp.dot(rows[:, dt:], head_s[...], preferred_element_type=F32),
            jnp.dot(rows[:, :dt], head_t[...], preferred_element_type=F32),
        ),
    )
    for half, s_half, u_half in halves:
        for j in range(tokens // 32):
            at = pl.ds(pl.multiple_of((2 * j + half) * 16, 16), 16)
            s_nat[at, :] = s_half[16 * j : 16 * j + 16]
            u_nat[at, :] = u_half[16 * j : 16 * j + 16]
    s_t = s_nat[...].T
    u_roll = u_nat[...].T
    order = lax.broadcasted_iota(jnp.int32, (tokens, tokens), 0)
    pick = jnp.where(order == route[...], 1.0, 0.0).astype(BF16)
    high = u_roll.astype(BF16)
    rest = u_roll - high.astype(F32)
    middle = rest.astype(BF16)
    low = (rest - middle.astype(F32)).astype(BF16)
    u_t = jnp.zeros_like(u_roll)
    for part in (low, middle, high):
        u_t = u_t + lax.dot_general(
            part, pick, (((1,), (1,)), ((), ())), preferred_element_type=F32
        )
    s_t_out[...] = s_t
    u_t_out[...] = u_t
    m_s = jnp.max(s_t, axis=0, keepdims=True)
    m_u = jnp.max(u_t, axis=0, keepdims=True)
    s_rel = s_t - m_s
    u_rel = u_t - m_u
    e_s = jnp.exp(s_rel)
    sum_s = jnp.sum(e_s, axis=0, keepdims=True)
    sum_u = jnp.sum(jnp.exp(u_rel), axis=0, keepdims=True)
    mean = jnp.sum(e_s * (s_rel - u_rel), axis=0, keepdims=True) / sum_s
    log_s = jnp.log(sum_s)
    log_u = jnp.log(sum_u)
    column = lax.broadcasted_iota(jnp.int32, s_t.shape, 0)
    hit = column == ids[...] - first_col
    apart = jnp.sum(jnp.where(hit, u_t - s_t, 0.0), axis=0, keepdims=True)
    store_stats(stats_out, (m_s + log_s, m_u + log_u, mean - log_s + log_u, apart))


def merge(parts):
    lse_s, lse_u = parts[:, 0:4], parts[:, 4:8]
    kl, apart = parts[:, 8:12], parts[:, 12:16]
    m_s = jnp.max(lse_s, axis=0)
    m_u = jnp.max(lse_u, axis=0)
    all_s = m_s + jnp.log(jnp.sum(jnp.exp(lse_s - m_s), axis=0))
    all_u = m_u + jnp.log(jnp.sum(jnp.exp(lse_u - m_u), axis=0))
    share = jnp.exp(lse_s - all_s)
    whole = jnp.sum(share * (kl + (lse_s - all_s) - (lse_u - all_u)), axis=0)
    return all_s, all_u, whole, jnp.sum(apart, axis=0)


def merge_kernel(parts, out):
    merged = jnp.concatenate(merge(parts[...]), axis=0)
    for i in range(out.shape[0]):
        out[i] = merged


def grad_kernel(
    where, lengths, parts, s_t, u_t, flags, own, other, kl_out, grad_out, dl_nat, dl_half
):
    core, group = where[0], where[2]
    tokens = dl_nat.shape[0]
    dt = own.shape[1] - grad_out.shape[0]

    def lanes(rows):
        return jnp.concatenate([rows[j : j + 1] for j in range(4)], axis=1)

    lse_s, lse_u, kl, apart = [lanes(v) for v in merge(parts[...])]
    slot = lax.broadcasted_iota(jnp.int32, (1, tokens), 1)
    length = jnp.zeros((1, tokens), jnp.int32)
    for w in range(lengths.shape[0]):
        length = jnp.where(slot // 16 == w, lengths[w], length)
    live = (slot % 16 < length).astype(F32)
    mixed = 1.0 / (0.2 * jnp.exp(apart - lse_u + lse_s) + 0.8)
    weight = jnp.where(flags[...] == 1, mixed, jnp.ones_like(mixed))
    kl_rows = live * kl
    mine = jnp.zeros((1, 16), F32)
    for w in range(lengths.shape[0]):
        mine = jnp.where(group == w, kl_rows[:, 16 * w : 16 * w + 16], mine)
    kl_out[...] = mine
    log_s = s_t[...] - lse_s
    gap = log_s - (u_t[...] - lse_u)
    d_t = (live * weight) * jnp.exp(log_s) * (gap - kl)
    dl_nat[...] = d_t.T
    for n, half in enumerate((core, 1 - core)):
        for j in range(tokens // 32):
            at = pl.ds(pl.multiple_of((2 * j + half) * 16, 16), 16)
            dl_half[n, 16 * j : 16 * j + 16, :] = dl_nat[at, :].astype(BF16)
    step = 512
    for f in range(0, grad_out.shape[0], step):
        total = jnp.zeros((grad_out.shape[1], step), F32)
        for n, rows in enumerate((own, other)):
            total = total + lax.dot_general(
                dl_half[n], rows[:, dt + f : dt + f + step], (((0,), (0,)), ((), ())),
                preferred_element_type=F32,
            )
        grad_out[f : f + step, :] = total.T.astype(BF16)


def on_device(
    student_hidden, teacher_rows, student_head, teacher_head, lengths, route, sampled_ids, mix_flags
):
    ny, nx, nz = lax.axis_size("y"), lax.axis_size("x"), lax.axis_size("z")
    core = lax.axis_index("c")
    group = (lax.axis_index("y") * nx + lax.axis_index("x")) * 2 + core
    grp_rows = student_hidden.shape[0]
    ds, vocab_dev = student_head.shape
    dt = teacher_head.shape[0]
    tokens = route.shape[0]
    half = tokens // 2
    first_col = (group * nz + lax.axis_index("z")) * vocab_dev
    where = jnp.stack([core, first_col, group]).astype(jnp.int32)

    local = jnp.concatenate([teacher_rows, student_hidden], axis=1)
    gathered = lax.all_to_all(jnp.broadcast_to(local, (nz,) + local.shape), "z", 0, 0)
    copies = pl.pallas_call(
        spread_kernel,
        out_shape=jax.ShapeDtypeStruct((ny * nx, grp_rows, dt + ds), BF16),
        in_specs=[VMEM], out_specs=VMEM, compiler_params=grant(8),
    )(gathered)
    own = lax.all_to_all(copies, ("y", "x"), 0, 0).reshape(half, dt + ds)
    other = lax.ppermute(own, "c", [(0, 1), (1, 0)])
    logits = jax.ShapeDtypeStruct((half, vocab_dev), F32)
    s_own, u_own = pl.pallas_call(
        half_kernel, out_shape=(logits, logits),
        in_specs=[VMEM] * 3, out_specs=(VMEM, VMEM), compiler_params=grant(8),
    )(own, student_head, teacher_head)
    whole = jax.ShapeDtypeStruct((vocab_dev, tokens), F32)
    block = (4 * tokens // 128, 128)
    s_t, u_t, stats = pl.pallas_call(
        stats_kernel,
        out_shape=(whole, whole, jax.ShapeDtypeStruct((2 * ny * nx,) + block, F32)),
        in_specs=[SMEM] + [VMEM] * 7, out_specs=(VMEM,) * 3,
        scratch_shapes=[pltpu.VMEM((tokens, vocab_dev), F32)] * 2, compiler_params=grant(8),
    )(where, other, student_head, teacher_head, s_own, u_own, route[None], sampled_ids[None])
    near = lax.all_to_all(stats, ("y", "x", "c"), 0, 0)
    merged = pl.pallas_call(
        merge_kernel,
        out_shape=jax.ShapeDtypeStruct((nz,) + block, F32),
        in_specs=[VMEM], out_specs=VMEM, compiler_params=grant(4),
    )(near)
    far = lax.all_to_all(merged, "z", 0, 0)
    kl_rows, head_grad = pl.pallas_call(
        grad_kernel,
        out_shape=(
            jax.ShapeDtypeStruct((1, grp_rows), F32),
            jax.ShapeDtypeStruct((ds, vocab_dev), BF16),
        ),
        in_specs=[SMEM] * 2 + [VMEM] * 6, out_specs=(VMEM,) * 2,
        scratch_shapes=[
            pltpu.VMEM((tokens, vocab_dev), F32), pltpu.VMEM((2, half, vocab_dev), BF16)
        ],
        compiler_params=grant(8),
    )(where, lengths, far, s_t, u_t, mix_flags[None], own, other)
    return kl_rows[0], head_grad


def solution(mesh):
    fine = Mesh(mesh.devices.reshape(4, 4, 2, 16), ("y", "x", "c", "z"))
    tok = ("y", "x", "c")
    every = tok + ("z",)
    in_specs = (P(tok, "z"), P(tok, "z"), P(None, every), P(None, every), P(), P(), P(), P())
    out_specs = (P(tok), P(None, every))
    return jax.shard_map(
        on_device, mesh=fine, in_specs=in_specs, out_specs=out_specs, check_vma=False
    )
```

```python
import jax
import jax.numpy as jnp
from jax import lax
from jax.experimental import pallas as pl
from jax.experimental.pallas import tpu as pltpu
from jax.sharding import Mesh, PartitionSpec as P

F32 = jnp.float32
BF16 = jnp.bfloat16
VMEM = pl.BlockSpec(memory_space=pltpu.VMEM)
SMEM = pl.BlockSpec(memory_space=pltpu.SMEM)
LIVE = 320
ROWS = 40
QT, QS = 64, 40


def grant(mib):
    return pltpu.CompilerParams(vmem_limit_bytes=mib * 1024 * 1024)


def dot(a, b, dims=((1,), (0,))):
    return lax.dot_general(a, b, (dims, ((), ())), preferred_element_type=F32)


def ranks(lengths, tokens):
    slot = lax.broadcasted_iota(jnp.int32, (1, tokens), 1)
    window, row = slot // 16, slot % 16
    rank = jnp.full((1, tokens), -1, jnp.int32)
    start = jnp.int32(0)
    for w in range(lengths.shape[0]):
        here = jnp.logical_and(window == w, row < lengths[w])
        rank = jnp.where(here, row + start, rank)
        start = start + lengths[w]
    return rank


def pick_kernel(where, lengths, near, route, out):
    chunk, quarter = where[3], where[4]
    tokens = route.shape[1]
    rows = near[...].reshape(tokens, near.shape[2])
    place = lax.broadcasted_iota(jnp.int32, (ROWS, tokens), 0) + chunk * ROWS
    pick_s = jnp.where(place == ranks(lengths, tokens), 1.0, 0.0).astype(BF16)
    order = lax.broadcasted_iota(jnp.int32, (tokens, tokens), 0)
    sent = jnp.where(order == route[...], 1.0, 0.0).astype(BF16)
    pick_t = dot(pick_s, sent).astype(BF16)
    teacher = dot(pick_t, rows[:, : 4 * QT])
    student = dot(pick_s, rows[:, 4 * QT :])
    part_t, part_s = teacher[:, :QT], student[:, :QS]
    for q in range(1, 4):
        part_t = jnp.where(quarter == q, teacher[:, QT * q : QT * q + QT], part_t)
        part_s = jnp.where(quarter == q, student[:, QS * q : QS * q + QS], part_s)
    block = jnp.concatenate([part_t, part_s], axis=1).astype(BF16)
    for i in range(out.shape[0]):
        out[i] = block


def spread_kernel(gathered, out):
    nz = gathered.shape[0]
    teacher = [gathered[z, :, :QT] for z in range(nz)]
    student = [gathered[z, :, QT:] for z in range(nz)]
    whole = jnp.concatenate(teacher + student, axis=1)
    for i in range(out.shape[0]):
        out[i] = whole


def logits_of(rows, head_s, head_t, core):
    dt = head_t.shape[1]
    s = sum(dot(rows[i, :, dt:], head_s[2 * core + i]) for i in range(2))
    u = sum(dot(rows[i, :, :dt], head_t[2 * core + i]) for i in range(2))
    return s, u


def half_kernel(where, rows, head_s, head_t, s_out, u_out):
    s_out[...], u_out[...] = logits_of(rows, head_s, head_t, where[0])


def stats_kernel(
    where, lengths, rows, head_s, head_t, s_own, u_own, ids, s_t_out, u_t_out, stats_out
):
    core, first_col = where[0], where[1]
    tokens = ids.shape[1]
    s, u = logits_of(rows, head_s, head_t, 1 - core)
    s_t = (s_own[...] + s).T
    u_t = (u_own[...] + u).T
    s_t_out[...] = s_t
    u_t_out[...] = u_t
    m_s = jnp.max(s_t, axis=0, keepdims=True)
    m_u = jnp.max(u_t, axis=0, keepdims=True)
    s_rel = s_t - m_s
    u_rel = u_t - m_u
    e_s = jnp.exp(s_rel)
    sum_s = jnp.sum(e_s, axis=0, keepdims=True)
    sum_u = jnp.sum(jnp.exp(u_rel), axis=0, keepdims=True)
    mean = jnp.sum(e_s * (s_rel - u_rel), axis=0, keepdims=True) / sum_s
    log_s = jnp.log(sum_s)
    log_u = jnp.log(sum_u)
    place = lax.broadcasted_iota(jnp.int32, (LIVE, tokens), 0)
    live = jnp.where(place == ranks(lengths, tokens), 1.0, 0.0).astype(BF16)
    all_ids = ids[...]
    digits = [all_ids % 64, all_ids // 64 % 64, all_ids // 4096]
    digits = jnp.concatenate([d.astype(F32) for d in digits] + [jnp.zeros((5, tokens), F32)], axis=0)
    digits = dot(digits.astype(BF16), live, ((1,), (1,))).astype(jnp.int32)
    wanted = digits[0:1] + 64 * digits[1:2] + 4096 * digits[2:3]
    column = lax.broadcasted_iota(jnp.int32, s_t.shape, 0)
    hit = column == wanted - first_col
    apart = jnp.sum(jnp.where(hit, u_t - s_t, 0.0), axis=0, keepdims=True)
    values = (m_s + log_s, m_u + log_u, mean - log_s + log_u, apart)
    lines = [v[:, 128 * j : 128 * j + 128] for v in values for j in range(2)]
    ends = jnp.concatenate([v[:, 256:LIVE] for v in values], axis=1)
    block = jnp.concatenate(lines + [ends[:, :128], ends[:, 128:], jnp.zeros((6, 128), F32)], axis=0)
    for i in range(stats_out.shape[0]):
        stats_out[i] = block


def merge(lse_s, lse_u, kl, apart):
    m_s = jnp.max(lse_s, axis=0)
    m_u = jnp.max(lse_u, axis=0)
    all_s = m_s + jnp.log(jnp.sum(jnp.exp(lse_s - m_s), axis=0))
    all_u = m_u + jnp.log(jnp.sum(jnp.exp(lse_u - m_u), axis=0))
    share = jnp.exp(lse_s - all_s)
    whole = jnp.sum(share * (kl + (lse_s - all_s) - (lse_u - all_u)), axis=0)
    return all_s, all_u, whole, jnp.sum(apart, axis=0)


def merge_lines(parts):
    main = merge(*(parts[:, 2 * k : 2 * k + 2] for k in range(4)))
    first, second = parts[:, 8:9], parts[:, 9:10]
    ends = merge(first[:, :, :64], first[:, :, 64:], second[:, :, :64], second[:, :, 64:])
    return main, ends


def merge_kernel(parts, out):
    main, ends = merge_lines(parts[...])
    tail = [jnp.concatenate(ends[:2], axis=1), jnp.concatenate(ends[2:], axis=1)]
    block = jnp.concatenate(list(main) + tail + [jnp.zeros((6, 128), F32)], axis=0)
    for i in range(out.shape[0]):
        out[i] = block


def grad_kernel(where, lengths, parts, s_t, u_t, flags, own, other, kl_out, grad_out):
    core, group = where[0], where[2]
    tokens = flags.shape[1]
    nz = grad_out.shape[0]
    dt = own.shape[2] - nz * QS
    main, ends = merge_lines(parts[...])
    lse_s, lse_u, kl, apart = [
        jnp.concatenate([m[0:1], m[1:2], e], axis=1) for m, e in zip(main, ends)
    ]
    place = lax.broadcasted_iota(jnp.int32, (LIVE, tokens), 0)
    live = jnp.where(place == ranks(lengths, tokens), 1.0, 0.0).astype(BF16)
    marks = jnp.broadcast_to(flags[...], (8, tokens)).astype(F32).astype(BF16)
    mark = dot(marks, live, ((1,), (1,)))[0:1]
    mixed = 1.0 / (0.2 * jnp.exp(apart - lse_u + lse_s) + 0.8)
    weight = jnp.where(mark > 0.5, mixed, jnp.ones_like(mixed))
    log_s = s_t[...] - lse_s
    gap = log_s - (u_t[...] - lse_u)
    d_t = (weight * jnp.exp(log_s) * (gap - kl)).astype(BF16)
    for half, rows in ((core, own), (1 - core, other)):
        for i in range(2):
            total = dot(d_t, rows[i, :, dt:]).T
            for z in range(nz):
                grad_out[z, 2 * half + i] = total[QS * z : QS * z + QS].astype(BF16)
    start = jnp.int32(0)
    for w in range(lengths.shape[0]):
        start = start + jnp.where(w < group, lengths[w], 0)
    row = lax.broadcasted_iota(jnp.int32, (16, LIVE), 0)
    column = lax.broadcasted_iota(jnp.int32, (16, LIVE), 1)
    mine = jnp.logical_and(column == row + start, row < lengths[group])
    mine = jnp.sum(jnp.where(mine, kl, 0.0), axis=1, keepdims=True)
    kl_out[...] = jnp.broadcast_to(mine, (16, 128)).T[0:1]


def on_device(
    student_hidden, teacher_rows, student_head, teacher_head, lengths, route, sampled_ids, mix_flags
):
    nz = lax.axis_size("z")
    core = lax.axis_index("c")
    x_hi, x_lo = lax.axis_index("xh"), lax.axis_index("xl")
    group = ((lax.axis_index("y") * 2 + x_hi) * 2 + x_lo) * 2 + core
    grp_rows = student_hidden.shape[0]
    ds, vocab_dev = student_head.shape
    dt = teacher_head.shape[0]
    quarter = (ds + dt) // 4
    first_col = (group * nz + lax.axis_index("z")) * vocab_dev
    where = [core, first_col, group, lax.axis_index("y") * 2 + x_hi, 2 * core + x_lo]
    where = jnp.stack(where).astype(jnp.int32)
    tok = ("y", "xh", "xl", "c")

    local = jnp.concatenate([teacher_rows, student_hidden], axis=1)
    near = lax.all_to_all(jnp.broadcast_to(local, (32,) + local.shape), tok, 0, 0)
    picked = pl.pallas_call(
        pick_kernel,
        out_shape=jax.ShapeDtypeStruct((nz, ROWS, QT + QS), BF16),
        in_specs=[SMEM] * 2 + [VMEM] * 2, out_specs=VMEM, compiler_params=grant(8),
    )(where, lengths, near, route[None])
    gathered = lax.all_to_all(picked, "z", 0, 0)
    copies = pl.pallas_call(
        spread_kernel,
        out_shape=jax.ShapeDtypeStruct((16, ROWS, quarter), BF16),
        in_specs=[VMEM], out_specs=VMEM, compiler_params=grant(8),
    )(gathered)
    own = lax.all_to_all(copies, ("xl", "y", "xh"), 0, 0).reshape(2, LIVE, quarter)
    other = lax.ppermute(own, "c", [(0, 1), (1, 0)])
    head_s = student_head.reshape(nz, 4, QS, vocab_dev).transpose(1, 0, 2, 3)
    head_s = head_s.reshape(4, ds // 4, vocab_dev)
    head_t = teacher_head.reshape(nz, 4, QT, vocab_dev).transpose(1, 0, 2, 3)
    head_t = head_t.reshape(4, dt // 4, vocab_dev)
    logits = jax.ShapeDtypeStruct((LIVE, vocab_dev), F32)
    s_own, u_own = pl.pallas_call(
        half_kernel, out_shape=(logits, logits),
        in_specs=[SMEM] + [VMEM] * 3, out_specs=(VMEM, VMEM), compiler_params=grant(8),
    )(where, own, head_s, head_t)
    whole = jax.ShapeDtypeStruct((vocab_dev, LIVE), F32)
    s_t, u_t, stats = pl.pallas_call(
        stats_kernel,
        out_shape=(whole, whole, jax.ShapeDtypeStruct((32, 16, 128), F32)),
        in_specs=[SMEM] * 2 + [VMEM] * 6, out_specs=(VMEM,) * 3, compiler_params=grant(8),
    )(where, lengths, other, head_s, head_t, s_own, u_own, sampled_ids[None])
    parts = lax.all_to_all(stats, tok, 0, 0)
    merged = pl.pallas_call(
        merge_kernel,
        out_shape=jax.ShapeDtypeStruct((nz, 16, 128), F32),
        in_specs=[VMEM], out_specs=VMEM, compiler_params=grant(4),
    )(parts)
    parts = lax.all_to_all(merged, "z", 0, 0)
    kl_rows, head_grad = pl.pallas_call(
        grad_kernel,
        out_shape=(
            jax.ShapeDtypeStruct((1, grp_rows), F32),
            jax.ShapeDtypeStruct((nz, 4, QS, vocab_dev), BF16),
        ),
        in_specs=[SMEM] * 2 + [VMEM] * 6, out_specs=(VMEM,) * 2, compiler_params=grant(8),
    )(where, lengths, parts, s_t, u_t, mix_flags[None], own, other)
    return kl_rows[0], head_grad.reshape(ds, vocab_dev)


def solution(mesh):
    axes = ("y", "xh", "xl", "c", "z")
    fine = Mesh(mesh.devices.reshape(4, 2, 2, 2, 16), axes)
    tok = axes[:4]
    in_specs = (P(tok, "z"), P(tok, "z"), P(None, axes), P(None, axes), P(), P(), P(), P())
    out_specs = (P(tok), P(None, axes))
    return jax.shard_map(
        on_device, mesh=fine, in_specs=in_specs, out_specs=out_specs, check_vma=False
    )
```

```python
import jax
import jax.numpy as jnp
from jax import lax
from jax.experimental import pallas as pl
from jax.experimental.pallas import tpu as pltpu
from jax.sharding import Mesh, PartitionSpec as P

F32 = jnp.float32
BF16 = jnp.bfloat16
VMEM = pl.BlockSpec(memory_space=pltpu.VMEM)
SMEM = pl.BlockSpec(memory_space=pltpu.SMEM)
LIVE = 320
ROWS = 40
QT, QS = 64, 40


def grant(mib):
    return pltpu.CompilerParams(vmem_limit_bytes=mib * 1024 * 1024)


def dot(a, b, dims=((1,), (0,))):
    return lax.dot_general(a, b, (dims, ((), ())), preferred_element_type=F32)


def ranks(table, tokens):
    slot = lax.broadcasted_iota(jnp.int32, (1, tokens), 1)
    window, row = slot // 16, slot % 16
    rank = jnp.full((1, tokens), -1, jnp.int32)
    start = jnp.int32(0)
    for w in range(table.shape[0] - 5):
        here = jnp.logical_and(window == w, row < table[5 + w])
        rank = jnp.where(here, row + start, rank)
        start = start + table[5 + w]
    return rank


def quarter_kernel(teacher_in, student_in, out, teacher, student, arrived):
    loads = [
        pltpu.make_async_copy(teacher_in, teacher, arrived.at[0]),
        pltpu.make_async_copy(student_in, student, arrived.at[1]),
    ]
    for load in loads:
        load.start()
    for load in loads:
        load.wait()
    blocks = []
    for q in range(4):
        part = [teacher[:, QT * q : QT * q + QT], student[:, QS * q : QS * q + QS]]
        blocks.append(jnp.concatenate(part, axis=1))
    for i in range(out.shape[0]):
        out[i] = blocks[2 * (i % 2) + i // 2 % 2]


def index_kernel(table, rows, pick_out, wanted_out, mark_out):
    chunk = table[3]
    tokens = rows.shape[1]
    rank = ranks(table, tokens)
    route, ids, flags = rows[0:1], rows[1:2], rows[2:3]
    place = lax.broadcasted_iota(jnp.int32, (ROWS, tokens), 0) + chunk * ROWS
    pick_s = jnp.where(place == rank, 1.0, 0.0).astype(BF16)
    order = lax.broadcasted_iota(jnp.int32, (tokens, tokens), 0)
    sent = jnp.where(order == route, 1.0, 0.0).astype(BF16)
    pick_out[0] = pick_s
    pick_out[1] = dot(pick_s, sent).astype(BF16)
    place = lax.broadcasted_iota(jnp.int32, (LIVE, tokens), 0)
    live = jnp.where(place == rank, 1.0, 0.0).astype(BF16)
    digits = [d.astype(F32) for d in (ids % 64, ids // 64 % 64, ids // 4096, flags)]
    digits = jnp.concatenate(digits + [jnp.zeros((4, tokens), F32)], axis=0)
    digits = dot(digits.astype(BF16), live, ((1,), (1,))).astype(jnp.int32)
    wanted_out[...] = digits[0:1] + 64 * digits[1:2] + 4096 * digits[2:3]
    mark_out[...] = digits[3:4]


def pick_kernel(near, pick, out):
    rows = near[...].reshape(near.shape[0] * near.shape[1], near.shape[2])
    block = jnp.concatenate([dot(pick[1], rows[:, :QT]), dot(pick[0], rows[:, QT:])], axis=1)
    block = block.astype(BF16)
    for i in range(out.shape[0]):
        out[i] = block


def spread_kernel(gathered, out):
    nz = gathered.shape[0]
    teacher = [gathered[z, :, :QT] for z in range(nz)]
    student = [gathered[z, :, QT:] for z in range(nz)]
    whole = jnp.concatenate(teacher + student, axis=1)
    for i in range(out.shape[0]):
        out[i] = whole


def logits_of(rows, head_s, head_t, core):
    dt = head_t.shape[1]
    s = sum(dot(rows[i, :, dt:], head_s[2 * core + i]) for i in range(2))
    u = sum(dot(rows[i, :, :dt], head_t[2 * core + i]) for i in range(2))
    return s, u


def half_kernel(where, rows, head_s, head_t, s_out, u_out):
    s_out[...], u_out[...] = logits_of(rows, head_s, head_t, where[0])


def stats_kernel(
    where, rows, head_s, head_t, s_own, u_own, wanted, s_t_out, u_t_out, stats_out
):
    core, first_col = where[0], where[1]
    s, u = logits_of(rows, head_s, head_t, 1 - core)
    s_t = (s_own[...] + s).T
    u_t = (u_own[...] + u).T
    s_t_out[...] = s_t
    u_t_out[...] = u_t
    m_s = jnp.max(s_t, axis=0, keepdims=True)
    m_u = jnp.max(u_t, axis=0, keepdims=True)
    s_rel = s_t - m_s
    u_rel = u_t - m_u
    e_s = jnp.exp(s_rel)
    sum_s = jnp.sum(e_s, axis=0, keepdims=True)
    sum_u = jnp.sum(jnp.exp(u_rel), axis=0, keepdims=True)
    mean = jnp.sum(e_s * (s_rel - u_rel), axis=0, keepdims=True) / sum_s
    log_s = jnp.log(sum_s)
    log_u = jnp.log(sum_u)
    column = lax.broadcasted_iota(jnp.int32, s_t.shape, 0)
    hit = column == wanted[...] - first_col
    apart = jnp.sum(jnp.where(hit, u_t - s_t, 0.0), axis=0, keepdims=True)
    block = jnp.concatenate([m_s + log_s, m_u + log_u, mean - log_s + log_u, apart], axis=1)
    for i in range(stats_out.shape[0]):
        stats_out[i] = block


def merge(parts):
    parts = parts[:, 0, :]
    lse_s, lse_u, kl, apart = [parts[:, LIVE * k : LIVE * k + LIVE] for k in range(4)]
    m_s = jnp.max(lse_s, axis=0, keepdims=True)
    m_u = jnp.max(lse_u, axis=0, keepdims=True)
    all_s = m_s + jnp.log(jnp.sum(jnp.exp(lse_s - m_s), axis=0, keepdims=True))
    all_u = m_u + jnp.log(jnp.sum(jnp.exp(lse_u - m_u), axis=0, keepdims=True))
    share = jnp.exp(lse_s - all_s)
    whole = share * (kl + (lse_s - all_s) - (lse_u - all_u))
    whole = jnp.sum(whole, axis=0, keepdims=True)
    return all_s, all_u, whole, jnp.sum(apart, axis=0, keepdims=True)


def merge_kernel(parts, out):
    block = jnp.concatenate(merge(parts[...]), axis=1)
    for i in range(out.shape[0]):
        out[i] = block


def grad_kernel(table, parts, s_t, u_t, mark, own, other, kl_out, grad_out):
    core, group = table[0], table[2]
    nz = grad_out.shape[0]
    dt = own.shape[2] - nz * QS
    lse_s, lse_u, kl, apart = merge(parts[...])
    mixed = 1.0 / (0.2 * jnp.exp(apart - lse_u + lse_s) + 0.8)
    weight = jnp.where(mark[...] == 1, mixed, jnp.ones_like(mixed))
    log_s = s_t[...] - lse_s
    gap = log_s - (u_t[...] - lse_u)
    d_t = (weight * jnp.exp(log_s) * (gap - kl)).astype(BF16)
    for half, rows in ((core, own), (1 - core, other)):
        for i in range(2):
            total = dot(d_t, rows[i, :, dt:]).T
            for z in range(nz):
                grad_out[z, 2 * half + i] = total[QS * z : QS * z + QS].astype(BF16)
    start = jnp.int32(0)
    for w in range(table.shape[0] - 5):
        start = start + jnp.where(w < group, table[5 + w], 0)
    row = lax.broadcasted_iota(jnp.int32, (16, LIVE), 0)
    column = lax.broadcasted_iota(jnp.int32, (16, LIVE), 1)
    mine = jnp.logical_and(column == row + start, row < table[5 + group])
    mine = jnp.sum(jnp.where(mine, kl, 0.0), axis=1, keepdims=True)
    kl_out[...] = jnp.broadcast_to(mine, (16, 128)).T[0:1]


def on_device(
    student_hidden, teacher_rows, student_head, teacher_head, lengths, route, sampled_ids, mix_flags
):
    nz = lax.axis_size("z")
    core = lax.axis_index("c")
    x_hi, x_lo = lax.axis_index("xh"), lax.axis_index("xl")
    group = ((lax.axis_index("y") * 2 + x_hi) * 2 + x_lo) * 2 + core
    grp_rows = student_hidden.shape[0]
    ds, vocab_dev = student_head.shape
    dt = teacher_head.shape[0]
    quarter = (ds + dt) // 4
    first_col = (group * nz + lax.axis_index("z")) * vocab_dev
    place = jnp.stack([core, first_col, group, lax.axis_index("y") * 2 + x_hi, x_lo])
    table = jnp.concatenate([place.astype(jnp.int32), lengths])
    rows = jnp.stack([route, sampled_ids, mix_flags])
    tok = ("y", "xh", "xl", "c")

    quarters = pl.pallas_call(
        quarter_kernel,
        out_shape=jax.ShapeDtypeStruct((32, grp_rows, QT + QS), BF16),
        in_specs=[pl.BlockSpec(memory_space=pltpu.HBM)] * 2, out_specs=VMEM,
        scratch_shapes=[
            pltpu.VMEM(teacher_rows.shape, BF16), pltpu.VMEM(student_hidden.shape, BF16),
            pltpu.SemaphoreType.DMA((2,)),
        ],
        compiler_params=grant(4),
    )(teacher_rows, student_hidden)
    near = lax.all_to_all(quarters, tok, 0, 0)
    per_row = jax.ShapeDtypeStruct((1, LIVE), jnp.int32)
    pick, wanted, mark = pl.pallas_call(
        index_kernel,
        out_shape=(jax.ShapeDtypeStruct((2, ROWS, route.shape[0]), BF16), per_row, per_row),
        in_specs=[SMEM, VMEM], out_specs=(VMEM,) * 3, compiler_params=grant(6),
    )(table, rows)
    picked = pl.pallas_call(
        pick_kernel,
        out_shape=jax.ShapeDtypeStruct((nz, ROWS, QT + QS), BF16),
        in_specs=[VMEM] * 2, out_specs=VMEM, compiler_params=grant(4),
    )(near, pick)
    gathered = lax.all_to_all(picked, "z", 0, 0)
    copies = pl.pallas_call(
        spread_kernel,
        out_shape=jax.ShapeDtypeStruct((16, ROWS, quarter), BF16),
        in_specs=[VMEM], out_specs=VMEM, compiler_params=grant(8),
    )(gathered)
    own = lax.all_to_all(copies, ("xl", "y", "xh"), 0, 0).reshape(2, LIVE, quarter)
    other = lax.ppermute(own, "c", [(0, 1), (1, 0)])
    head_s = student_head.reshape(nz, 4, QS, vocab_dev).transpose(1, 0, 2, 3)
    head_s = head_s.reshape(4, ds // 4, vocab_dev)
    head_t = teacher_head.reshape(nz, 4, QT, vocab_dev).transpose(1, 0, 2, 3)
    head_t = head_t.reshape(4, dt // 4, vocab_dev)
    logits = jax.ShapeDtypeStruct((LIVE, vocab_dev), F32)
    s_own, u_own = pl.pallas_call(
        half_kernel, out_shape=(logits, logits),
        in_specs=[SMEM] + [VMEM] * 3, out_specs=(VMEM, VMEM), compiler_params=grant(8),
    )(table, own, head_s, head_t)
    whole = jax.ShapeDtypeStruct((vocab_dev, LIVE), F32)
    s_t, u_t, stats = pl.pallas_call(
        stats_kernel,
        out_shape=(whole, whole, jax.ShapeDtypeStruct((32, 1, 4 * LIVE), F32)),
        in_specs=[SMEM] + [VMEM] * 6, out_specs=(VMEM,) * 3, compiler_params=grant(8),
    )(table, other, head_s, head_t, s_own, u_own, wanted)
    parts = lax.all_to_all(stats, tok, 0, 0)
    merged = pl.pallas_call(
        merge_kernel,
        out_shape=jax.ShapeDtypeStruct((nz, 1, 4 * LIVE), F32),
        in_specs=[VMEM], out_specs=VMEM, compiler_params=grant(4),
    )(parts)
    parts = lax.all_to_all(merged, "z", 0, 0)
    kl_rows, head_grad = pl.pallas_call(
        grad_kernel,
        out_shape=(
            jax.ShapeDtypeStruct((1, grp_rows), F32),
            jax.ShapeDtypeStruct((nz, 4, QS, vocab_dev), BF16),
        ),
        in_specs=[SMEM] + [VMEM] * 6, out_specs=(VMEM,) * 2, compiler_params=grant(8),
    )(table, parts, s_t, u_t, mark, own, other)
    return kl_rows[0], head_grad.reshape(ds, vocab_dev)


def solution(mesh):
    axes = ("y", "xh", "xl", "c", "z")
    fine = Mesh(mesh.devices.reshape(4, 2, 2, 2, 16), axes)
    tok = axes[:4]
    in_specs = (P(tok, "z"), P(tok, "z"), P(None, axes), P(None, axes), P(), P(), P(), P())
    out_specs = (P(tok), P(None, axes))
    return jax.shard_map(
        on_device, mesh=fine, in_specs=in_specs, out_specs=out_specs, check_vma=False
    )
```

```python
import jax
import jax.numpy as jnp
from jax import lax
from jax.experimental import pallas as pl
from jax.experimental.pallas import tpu as pltpu
from jax.sharding import Mesh, PartitionSpec as P

F32 = jnp.float32
BF16 = jnp.bfloat16
VMEM = pl.BlockSpec(memory_space=pltpu.VMEM)
SMEM = pl.BlockSpec(memory_space=pltpu.SMEM)
LIVE = 320
ROWS = 40
QT, QS = 64, 40


def grant(mib):
    return pltpu.CompilerParams(vmem_limit_bytes=mib * 1024 * 1024)


def dot(a, b, dims=((1,), (0,))):
    return lax.dot_general(a, b, (dims, ((), ())), preferred_element_type=F32)


def ranks(table, tokens):
    slot = lax.broadcasted_iota(jnp.int32, (1, tokens), 1)
    window, row = slot // 16, slot % 16
    rank = jnp.full((1, tokens), -1, jnp.int32)
    start = jnp.int32(0)
    for w in range(table.shape[0] - 5):
        here = jnp.logical_and(window == w, row < table[5 + w])
        rank = jnp.where(here, row + start, rank)
        start = start + table[5 + w]
    return rank


def quarter_kernel(local, out):
    teacher, student = local[:, : 4 * QT], local[:, 4 * QT :]
    blocks = []
    for q in range(4):
        part = [teacher[:, QT * q : QT * q + QT], student[:, QS * q : QS * q + QS]]
        blocks.append(jnp.concatenate(part, axis=1))
    for i in range(out.shape[0]):
        out[i] = blocks[2 * (i % 2) + i // 2 % 2]


def index_kernel(table, rows, pick_out, wanted_out, mark_out):
    chunk = table[3]
    tokens = rows.shape[1]
    rank = ranks(table, tokens)
    route, ids, flags = rows[0:1], rows[1:2], rows[2:3]
    place = lax.broadcasted_iota(jnp.int32, (ROWS, tokens), 0) + chunk * ROWS
    pick_s = jnp.where(place == rank, 1.0, 0.0).astype(BF16)
    order = lax.broadcasted_iota(jnp.int32, (tokens, tokens), 0)
    sent = jnp.where(order == route, 1.0, 0.0).astype(BF16)
    pick_out[0] = pick_s
    pick_out[1] = dot(pick_s, sent).astype(BF16)
    place = lax.broadcasted_iota(jnp.int32, (LIVE, tokens), 0)
    live = jnp.where(place == rank, 1.0, 0.0).astype(BF16)
    digits = [d.astype(F32) for d in (ids % 64, ids // 64 % 64, ids // 4096, flags)]
    digits = jnp.concatenate(digits + [jnp.zeros((4, tokens), F32)], axis=0)
    digits = dot(digits.astype(BF16), live, ((1,), (1,))).astype(jnp.int32)
    wanted_out[...] = digits[0:1] + 64 * digits[1:2] + 4096 * digits[2:3]
    mark_out[...] = digits[3:4]


def pick_kernel(near, pick, out):
    rows = near[...].reshape(near.shape[0] * near.shape[1], near.shape[2])
    block = jnp.concatenate([dot(pick[1], rows[:, :QT]), dot(pick[0], rows[:, QT:])], axis=1)
    block = block.astype(BF16)
    for i in range(out.shape[0]):
        out[i] = block


def spread_kernel(gathered, out):
    nz = gathered.shape[0]
    teacher = [gathered[z, :, :QT] for z in range(nz)]
    student = [gathered[z, :, QT:] for z in range(nz)]
    whole = jnp.concatenate(teacher + student, axis=1)
    for i in range(out.shape[0]):
        out[i] = whole


def logits_of(rows, head_s, head_t, core):
    dt = head_t.shape[1]
    s = sum(dot(rows[i, :, dt:], head_s[2 * core + i]) for i in range(2))
    u = sum(dot(rows[i, :, :dt], head_t[2 * core + i]) for i in range(2))
    return s, u


def half_kernel(where, rows, head_s, head_t, s_out, u_out, turned):
    s_out[...], u_out[...] = logits_of(rows, head_s, head_t, where[0])
    for i in range(2):
        turned[i] = rows[i, :, head_t.shape[1] :].T


def stats_kernel(
    where, rows, head_s, head_t, s_own, u_own, wanted, s_t_out, u_t_out, stats_out
):
    core, first_col = where[0], where[1]
    s, u = logits_of(rows, head_s, head_t, 1 - core)
    s_t = (s_own[...] + s).T
    u_t = (u_own[...] + u).T
    s_t_out[...] = s_t
    u_t_out[...] = u_t
    m_s = jnp.max(s_t, axis=0, keepdims=True)
    m_u = jnp.max(u_t, axis=0, keepdims=True)
    s_rel = s_t - m_s
    u_rel = u_t - m_u
    e_s = jnp.exp(s_rel)
    sum_s = jnp.sum(e_s, axis=0, keepdims=True)
    sum_u = jnp.sum(jnp.exp(u_rel), axis=0, keepdims=True)
    mean = jnp.sum(e_s * (s_rel - u_rel), axis=0, keepdims=True) / sum_s
    log_s = jnp.log(sum_s)
    log_u = jnp.log(sum_u)
    column = lax.broadcasted_iota(jnp.int32, s_t.shape, 0)
    hit = column == wanted[...] - first_col
    apart = jnp.sum(jnp.where(hit, u_t - s_t, 0.0), axis=0, keepdims=True)
    block = jnp.concatenate([m_s + log_s, m_u + log_u, mean - log_s + log_u, apart], axis=1)
    for i in range(stats_out.shape[0]):
        stats_out[i] = block


def merge(parts):
    parts = parts[:, 0, :]
    lse_s, lse_u, kl, apart = [parts[:, LIVE * k : LIVE * k + LIVE] for k in range(4)]
    m_s = jnp.max(lse_s, axis=0, keepdims=True)
    m_u = jnp.max(lse_u, axis=0, keepdims=True)
    all_s = m_s + jnp.log(jnp.sum(jnp.exp(lse_s - m_s), axis=0, keepdims=True))
    all_u = m_u + jnp.log(jnp.sum(jnp.exp(lse_u - m_u), axis=0, keepdims=True))
    share = jnp.exp(lse_s - all_s)
    whole = share * (kl + (lse_s - all_s) - (lse_u - all_u))
    whole = jnp.sum(whole, axis=0, keepdims=True)
    return all_s, all_u, whole, jnp.sum(apart, axis=0, keepdims=True)


def merge_kernel(parts, out):
    block = jnp.concatenate(merge(parts[...]), axis=1)
    for i in range(out.shape[0]):
        out[i] = block


def grad_kernel(
    table, parts, s_t, u_t, mark, turned, other, kl_out, grad_out, ready, sent
):
    core, group = table[0], table[2]
    nz = grad_out.shape[0]
    dt = other.shape[2] - nz * QS
    lse_s, lse_u, kl, apart = merge(parts[...])
    mixed = 1.0 / (0.2 * jnp.exp(apart - lse_u + lse_s) + 0.8)
    weight = jnp.where(mark[...] == 1, mixed, jnp.ones_like(mixed))
    log_s = s_t[...] - lse_s
    gap = log_s - (u_t[...] - lse_u)
    d_t = (weight * jnp.exp(log_s) * (gap - kl)).astype(BF16)
    leaving = []
    for n in range(4):
        if n < 2:
            block = dot(turned[n], d_t, ((1,), (1,)))
        else:
            block = dot(d_t, other[n - 2, :, dt:]).T
        for z in range(nz):
            ready[n, z] = block[QS * z : QS * z + QS].astype(BF16)
        half = core if n < 2 else 1 - core
        copy = pltpu.make_async_copy(ready.at[n], grad_out.at[:, 2 * half + n % 2], sent.at[n])
        copy.start()
        leaving.append(copy)
    start = jnp.int32(0)
    for w in range(table.shape[0] - 5):
        start = start + jnp.where(w < group, table[5 + w], 0)
    row = lax.broadcasted_iota(jnp.int32, (16, LIVE), 0)
    column = lax.broadcasted_iota(jnp.int32, (16, LIVE), 1)
    mine = jnp.logical_and(column == row + start, row < table[5 + group])
    mine = jnp.sum(jnp.where(mine, kl, 0.0), axis=1, keepdims=True)
    kl_out[...] = jnp.broadcast_to(mine, (16, 128)).T[0:1]
    for copy in leaving:
        copy.wait()


def on_device(
    student_hidden, teacher_rows, student_head, teacher_head, lengths, route, sampled_ids, mix_flags
):
    nz = lax.axis_size("z")
    core = lax.axis_index("c")
    x_hi, x_lo = lax.axis_index("xh"), lax.axis_index("xl")
    group = ((lax.axis_index("y") * 2 + x_hi) * 2 + x_lo) * 2 + core
    grp_rows = student_hidden.shape[0]
    ds, vocab_dev = student_head.shape
    dt = teacher_head.shape[0]
    quarter = (ds + dt) // 4
    first_col = (group * nz + lax.axis_index("z")) * vocab_dev
    place = jnp.stack([core, first_col, group, lax.axis_index("y") * 2 + x_hi, x_lo])
    table = jnp.concatenate([place.astype(jnp.int32), lengths])
    rows = jnp.stack([route, sampled_ids, mix_flags])
    tok = ("y", "xh", "xl", "c")

    quarters = pl.pallas_call(
        quarter_kernel,
        out_shape=jax.ShapeDtypeStruct((32, grp_rows, QT + QS), BF16),
        in_specs=[VMEM], out_specs=VMEM, compiler_params=grant(4),
    )(jnp.concatenate([teacher_rows, student_hidden], axis=1))
    near = lax.all_to_all(quarters, tok, 0, 0)
    per_row = jax.ShapeDtypeStruct((1, LIVE), jnp.int32)
    pick, wanted, mark = pl.pallas_call(
        index_kernel,
        out_shape=(jax.ShapeDtypeStruct((2, ROWS, route.shape[0]), BF16), per_row, per_row),
        in_specs=[SMEM, VMEM], out_specs=(VMEM,) * 3, compiler_params=grant(6),
    )(table, rows)
    picked = pl.pallas_call(
        pick_kernel,
        out_shape=jax.ShapeDtypeStruct((nz, ROWS, QT + QS), BF16),
        in_specs=[VMEM] * 2, out_specs=VMEM, compiler_params=grant(4),
    )(near, pick)
    gathered = lax.all_to_all(picked, "z", 0, 0)
    copies = pl.pallas_call(
        spread_kernel,
        out_shape=jax.ShapeDtypeStruct((16, ROWS, quarter), BF16),
        in_specs=[VMEM], out_specs=VMEM, compiler_params=grant(8),
    )(gathered)
    own = lax.all_to_all(copies, ("xl", "y", "xh"), 0, 0).reshape(2, LIVE, quarter)
    other = lax.ppermute(own, "c", [(0, 1), (1, 0)])
    head_s = student_head.reshape(nz, 4, QS, vocab_dev).transpose(1, 0, 2, 3)
    head_s = head_s.reshape(4, ds // 4, vocab_dev)
    head_t = teacher_head.reshape(nz, 4, QT, vocab_dev).transpose(1, 0, 2, 3)
    head_t = head_t.reshape(4, dt // 4, vocab_dev)
    logits = jax.ShapeDtypeStruct((LIVE, vocab_dev), F32)
    turned = jax.ShapeDtypeStruct((2, ds // 4, LIVE), BF16)
    s_own, u_own, turned = pl.pallas_call(
        half_kernel, out_shape=(logits, logits, turned),
        in_specs=[SMEM] + [VMEM] * 3, out_specs=(VMEM,) * 3, compiler_params=grant(8),
    )(table, own, head_s, head_t)
    whole = jax.ShapeDtypeStruct((vocab_dev, LIVE), F32)
    s_t, u_t, stats = pl.pallas_call(
        stats_kernel,
        out_shape=(whole, whole, jax.ShapeDtypeStruct((32, 1, 4 * LIVE), F32)),
        in_specs=[SMEM] + [VMEM] * 6, out_specs=(VMEM,) * 3, compiler_params=grant(8),
    )(table, other, head_s, head_t, s_own, u_own, wanted)
    parts = lax.all_to_all(stats, tok, 0, 0)
    merged = pl.pallas_call(
        merge_kernel,
        out_shape=jax.ShapeDtypeStruct((nz, 1, 4 * LIVE), F32),
        in_specs=[VMEM], out_specs=VMEM, compiler_params=grant(4),
    )(parts)
    parts = lax.all_to_all(merged, "z", 0, 0)
    kl_rows, head_grad = pl.pallas_call(
        grad_kernel,
        out_shape=(
            jax.ShapeDtypeStruct((1, grp_rows), F32),
            jax.ShapeDtypeStruct((nz, 4, QS, vocab_dev), BF16),
        ),
        in_specs=[SMEM] + [VMEM] * 6,
        out_specs=(VMEM, pl.BlockSpec(memory_space=pl.ANY)),
        scratch_shapes=[
            pltpu.VMEM((4, nz, QS, vocab_dev), BF16), pltpu.SemaphoreType.DMA((4,))
        ],
        compiler_params=grant(8),
    )(table, parts, s_t, u_t, mark, turned, other)
    return kl_rows[0], head_grad.reshape(ds, vocab_dev)


def solution(mesh):
    axes = ("y", "xh", "xl", "c", "z")
    fine = Mesh(mesh.devices.reshape(4, 2, 2, 2, 16), axes)
    tok = axes[:4]
    in_specs = (P(tok, "z"), P(tok, "z"), P(None, axes), P(None, axes), P(), P(), P(), P())
    out_specs = (P(tok), P(None, axes))
    return jax.shard_map(
        on_device, mesh=fine, in_specs=in_specs, out_specs=out_specs, check_vma=False
    )
```

```python
import jax
import jax.numpy as jnp
from jax import lax
from jax.experimental import pallas as pl
from jax.experimental.pallas import tpu as pltpu
from jax.sharding import Mesh, PartitionSpec as P

F32 = jnp.float32
BF16 = jnp.bfloat16
VMEM = pl.BlockSpec(memory_space=pltpu.VMEM)
SMEM = pl.BlockSpec(memory_space=pltpu.SMEM)
LIVE = 320
ROWS = 40
QT, QS = 64, 40


def grant(mib):
    return pltpu.CompilerParams(vmem_limit_bytes=mib * 1024 * 1024)


def dot(a, b, dims=((1,), (0,))):
    return lax.dot_general(a, b, (dims, ((), ())), preferred_element_type=F32)


def ranks(table, tokens):
    slot = lax.broadcasted_iota(jnp.int32, (1, tokens), 1)
    window, row = slot // 16, slot % 16
    rank = jnp.full((1, tokens), -1, jnp.int32)
    start = jnp.int32(0)
    for w in range(table.shape[0] - 5):
        here = jnp.logical_and(window == w, row < table[5 + w])
        rank = jnp.where(here, row + start, rank)
        start = start + table[5 + w]
    return rank


def quarter_kernel(local, out):
    teacher, student = local[:, : 4 * QT], local[:, 4 * QT :]
    blocks = []
    for q in range(4):
        part = [teacher[:, QT * q : QT * q + QT], student[:, QS * q : QS * q + QS]]
        blocks.append(jnp.concatenate(part, axis=1))
    for i in range(out.shape[0]):
        out[i] = blocks[2 * (i % 2) + i // 2 % 2]


def index_kernel(table, rows, pick_out, wanted_out, mark_out):
    chunk = table[3]
    tokens = rows.shape[1]
    rank = ranks(table, tokens)
    route, ids, flags = rows[0:1], rows[1:2], rows[2:3]
    place = lax.broadcasted_iota(jnp.int32, (ROWS, tokens), 0) + chunk * ROWS
    pick_s = jnp.where(place == rank, 1.0, 0.0).astype(BF16)
    order = lax.broadcasted_iota(jnp.int32, (tokens, tokens), 0)
    sent = jnp.where(order == route, 1.0, 0.0).astype(BF16)
    pick_out[0] = pick_s
    pick_out[1] = dot(pick_s, sent).astype(BF16)
    place = lax.broadcasted_iota(jnp.int32, (LIVE, tokens), 0)
    live = jnp.where(place == rank, 1.0, 0.0).astype(BF16)
    digits = [d.astype(F32) for d in (ids % 64, ids // 64 % 64, ids // 4096, flags)]
    digits = jnp.concatenate(digits + [jnp.zeros((4, tokens), F32)], axis=0)
    digits = dot(digits.astype(BF16), live, ((1,), (1,))).astype(jnp.int32)
    wanted_out[...] = digits[0:1] + 64 * digits[1:2] + 4096 * digits[2:3]
    mark_out[...] = digits[3:4]


def pick_kernel(near, pick, out):
    rows = near[...].reshape(near.shape[0] * near.shape[1], near.shape[2])
    block = jnp.concatenate([dot(pick[1], rows[:, :QT]), dot(pick[0], rows[:, QT:])], axis=1)
    block = block.astype(BF16)
    for i in range(out.shape[0]):
        out[i] = block


def spread_kernel(gathered, out):
    nz = gathered.shape[0]
    teacher = [gathered[z, :, :QT] for z in range(nz)]
    student = [gathered[z, :, QT:] for z in range(nz)]
    whole = jnp.concatenate(teacher + student, axis=1)
    for i in range(out.shape[0]):
        out[i] = whole


def logits_of(rows, head_s, head_t, core):
    dt = head_t.shape[1]
    s = sum(dot(rows[i, :, dt:], head_s[2 * core + i]) for i in range(2))
    u = sum(dot(rows[i, :, :dt], head_t[2 * core + i]) for i in range(2))
    return s, u


def half_kernel(where, rows, head_s, head_t, s_out, u_out, turned):
    s_out[...], u_out[...] = logits_of(rows, head_s, head_t, where[0])
    for i in range(2):
        turned[i] = rows[i, :, head_t.shape[1] :].T


def stats_kernel(
    where, rows, head_s, head_t, s_own, u_own, wanted, s_t_out, u_t_out, stats_out
):
    core, first_col = where[0], where[1]
    s, u = logits_of(rows, head_s, head_t, 1 - core)
    s_t = (s_own[...] + s).T
    u_t = (u_own[...] + u).T
    s_t_out[...] = s_t
    u_t_out[...] = u_t
    m_s = jnp.max(s_t, axis=0, keepdims=True)
    m_u = jnp.max(u_t, axis=0, keepdims=True)
    s_rel = s_t - m_s
    u_rel = u_t - m_u
    e_s = jnp.exp(s_rel)
    sum_s = jnp.sum(e_s, axis=0, keepdims=True)
    sum_u = jnp.sum(jnp.exp(u_rel), axis=0, keepdims=True)
    mean = jnp.sum(e_s * (s_rel - u_rel), axis=0, keepdims=True) / sum_s
    log_s = jnp.log(sum_s)
    log_u = jnp.log(sum_u)
    column = lax.broadcasted_iota(jnp.int32, s_t.shape, 0)
    hit = column == wanted[...] - first_col
    apart = jnp.sum(jnp.where(hit, u_t - s_t, 0.0), axis=0, keepdims=True)
    block = jnp.concatenate([m_s + log_s, m_u + log_u, mean - log_s + log_u, apart], axis=1)
    for i in range(stats_out.shape[0]):
        stats_out[i] = block


def merge(parts):
    parts = parts[:, 0, :]
    lse_s, lse_u, kl, apart = [parts[:, LIVE * k : LIVE * k + LIVE] for k in range(4)]
    m_s = jnp.max(lse_s, axis=0, keepdims=True)
    m_u = jnp.max(lse_u, axis=0, keepdims=True)
    all_s = m_s + jnp.log(jnp.sum(jnp.exp(lse_s - m_s), axis=0, keepdims=True))
    all_u = m_u + jnp.log(jnp.sum(jnp.exp(lse_u - m_u), axis=0, keepdims=True))
    share = jnp.exp(lse_s - all_s)
    whole = share * (kl + (lse_s - all_s) - (lse_u - all_u))
    whole = jnp.sum(whole, axis=0, keepdims=True)
    return all_s, all_u, whole, jnp.sum(apart, axis=0, keepdims=True)


def merge_kernel(parts, out):
    block = jnp.concatenate(merge(parts[...]), axis=1)
    for i in range(out.shape[0]):
        out[i] = block


def grad_kernel(
    table, parts, s_t, u_t, mark, turned, other, kl_out, grad_out
):
    core, group = table[0], table[2]
    nz = grad_out.shape[0]
    dt = other.shape[2] - nz * QS
    lse_s, lse_u, kl, apart = merge(parts[...])
    mixed = 1.0 / (0.2 * jnp.exp(apart - lse_u + lse_s) + 0.8)
    weight = jnp.where(mark[...] == 1, mixed, jnp.ones_like(mixed))
    log_s = s_t[...] - lse_s
    gap = log_s - (u_t[...] - lse_u)
    d = (weight * jnp.exp(log_s) * (gap - kl)).T.astype(BF16)
    for n in range(4):
        if n < 2:
            block = dot(turned[n], d)
        else:
            block = dot(other[n - 2, :, dt:], d, ((0,), (0,)))
        half = core if n < 2 else 1 - core
        for z in range(nz):
            grad_out[z, 2 * half + n % 2] = block[QS * z : QS * z + QS].astype(BF16)
    start = jnp.int32(0)
    for w in range(table.shape[0] - 5):
        start = start + jnp.where(w < group, table[5 + w], 0)
    row = lax.broadcasted_iota(jnp.int32, (16, LIVE), 0)
    column = lax.broadcasted_iota(jnp.int32, (16, LIVE), 1)
    mine = jnp.logical_and(column == row + start, row < table[5 + group])
    mine = jnp.sum(jnp.where(mine, kl, 0.0), axis=1, keepdims=True)
    kl_out[...] = jnp.broadcast_to(mine, (16, 128)).T[0:1]


def on_device(
    student_hidden, teacher_rows, student_head, teacher_head, lengths, route, sampled_ids, mix_flags
):
    nz = lax.axis_size("z")
    core = lax.axis_index("c")
    x_hi, x_lo = lax.axis_index("xh"), lax.axis_index("xl")
    group = ((lax.axis_index("y") * 2 + x_hi) * 2 + x_lo) * 2 + core
    grp_rows = student_hidden.shape[0]
    ds, vocab_dev = student_head.shape
    dt = teacher_head.shape[0]
    quarter = (ds + dt) // 4
    first_col = (group * nz + lax.axis_index("z")) * vocab_dev
    place = jnp.stack([core, first_col, group, lax.axis_index("y") * 2 + x_hi, x_lo])
    table = jnp.concatenate([place.astype(jnp.int32), lengths])
    rows = jnp.stack([route, sampled_ids, mix_flags])
    tok = ("y", "xh", "xl", "c")

    quarters = pl.pallas_call(
        quarter_kernel,
        out_shape=jax.ShapeDtypeStruct((32, grp_rows, QT + QS), BF16),
        in_specs=[VMEM], out_specs=VMEM, compiler_params=grant(4),
    )(jnp.concatenate([teacher_rows, student_hidden], axis=1))
    near = lax.all_to_all(quarters, tok, 0, 0)
    per_row = jax.ShapeDtypeStruct((1, LIVE), jnp.int32)
    pick, wanted, mark = pl.pallas_call(
        index_kernel,
        out_shape=(jax.ShapeDtypeStruct((2, ROWS, route.shape[0]), BF16), per_row, per_row),
        in_specs=[SMEM, VMEM], out_specs=(VMEM,) * 3, compiler_params=grant(6),
    )(table, rows)
    picked = pl.pallas_call(
        pick_kernel,
        out_shape=jax.ShapeDtypeStruct((nz, ROWS, QT + QS), BF16),
        in_specs=[VMEM] * 2, out_specs=VMEM, compiler_params=grant(4),
    )(near, pick)
    gathered = lax.all_to_all(picked, "z", 0, 0)
    copies = pl.pallas_call(
        spread_kernel,
        out_shape=jax.ShapeDtypeStruct((16, ROWS, quarter), BF16),
        in_specs=[VMEM], out_specs=VMEM, compiler_params=grant(8),
    )(gathered)
    own = lax.all_to_all(copies, ("xl", "y", "xh"), 0, 0).reshape(2, LIVE, quarter)
    other = lax.ppermute(own, "c", [(0, 1), (1, 0)])
    head_s = student_head.reshape(nz, 4, QS, vocab_dev).transpose(1, 0, 2, 3)
    head_s = head_s.reshape(4, ds // 4, vocab_dev)
    head_t = teacher_head.reshape(nz, 4, QT, vocab_dev).transpose(1, 0, 2, 3)
    head_t = head_t.reshape(4, dt // 4, vocab_dev)
    logits = jax.ShapeDtypeStruct((LIVE, vocab_dev), F32)
    turned = jax.ShapeDtypeStruct((2, ds // 4, LIVE), BF16)
    s_own, u_own, turned = pl.pallas_call(
        half_kernel, out_shape=(logits, logits, turned),
        in_specs=[SMEM] + [VMEM] * 3, out_specs=(VMEM,) * 3, compiler_params=grant(8),
    )(table, own, head_s, head_t)
    whole = jax.ShapeDtypeStruct((vocab_dev, LIVE), F32)
    s_t, u_t, stats = pl.pallas_call(
        stats_kernel,
        out_shape=(whole, whole, jax.ShapeDtypeStruct((32, 1, 4 * LIVE), F32)),
        in_specs=[SMEM] + [VMEM] * 6, out_specs=(VMEM,) * 3, compiler_params=grant(8),
    )(table, other, head_s, head_t, s_own, u_own, wanted)
    parts = lax.all_to_all(stats, tok, 0, 0)
    merged = pl.pallas_call(
        merge_kernel,
        out_shape=jax.ShapeDtypeStruct((nz, 1, 4 * LIVE), F32),
        in_specs=[VMEM], out_specs=VMEM, compiler_params=grant(4),
    )(parts)
    parts = lax.all_to_all(merged, "z", 0, 0)
    kl_rows, head_grad = pl.pallas_call(
        grad_kernel,
        out_shape=(
            jax.ShapeDtypeStruct((1, grp_rows), F32),
            jax.ShapeDtypeStruct((nz, 4, QS, vocab_dev), BF16),
        ),
        in_specs=[SMEM] + [VMEM] * 6,
        out_specs=(VMEM,) * 2,
        compiler_params=grant(8),
    )(table, parts, s_t, u_t, mark, turned, other)
    return kl_rows[0], head_grad.reshape(ds, vocab_dev)


def solution(mesh):
    axes = ("y", "xh", "xl", "c", "z")
    fine = Mesh(mesh.devices.reshape(4, 2, 2, 2, 16), axes)
    tok = axes[:4]
    in_specs = (P(tok, "z"), P(tok, "z"), P(None, axes), P(None, axes), P(), P(), P(), P())
    out_specs = (P(tok), P(None, axes))
    return jax.shard_map(
        on_device, mesh=fine, in_specs=in_specs, out_specs=out_specs, check_vma=False
    )
```

```python
import jax
import jax.numpy as jnp
from jax import lax
from jax.experimental import pallas as pl
from jax.experimental.pallas import tpu as pltpu
from jax.sharding import Mesh, PartitionSpec as P

F32 = jnp.float32
BF16 = jnp.bfloat16
VMEM = pl.BlockSpec(memory_space=pltpu.VMEM)
SMEM = pl.BlockSpec(memory_space=pltpu.SMEM)
LIVE = 320
ROWS = 40
QT, QS = 64, 40


def grant(mib):
    return pltpu.CompilerParams(vmem_limit_bytes=mib * 1024 * 1024)


def dot(a, b, dims=((1,), (0,))):
    return lax.dot_general(a, b, (dims, ((), ())), preferred_element_type=F32)


def ranks(table, tokens):
    slot = lax.broadcasted_iota(jnp.int32, (1, tokens), 1)
    window, row = slot // 16, slot % 16
    rank = jnp.full((1, tokens), -1, jnp.int32)
    start = jnp.int32(0)
    for w in range(table.shape[0] - 5):
        here = jnp.logical_and(window == w, row < table[5 + w])
        rank = jnp.where(here, row + start, rank)
        start = start + table[5 + w]
    return rank


def quarter_kernel(local, out):
    teacher, student = local[:, : 4 * QT], local[:, 4 * QT :]
    blocks = []
    for q in range(4):
        part = [teacher[:, QT * q : QT * q + QT], student[:, QS * q : QS * q + QS]]
        blocks.append(jnp.concatenate(part, axis=1))
    for i in range(out.shape[0]):
        out[i] = blocks[2 * (i % 2) + i // 2 % 2]


def index_kernel(table, rows, pick_out, wanted_out, mark_out):
    chunk = table[3]
    tokens = rows.shape[1]
    rank = ranks(table, tokens)
    route, ids, flags = rows[0:1], rows[1:2], rows[2:3]
    place = lax.broadcasted_iota(jnp.int32, (ROWS, tokens), 0) + chunk * ROWS
    pick_s = jnp.where(place == rank, 1.0, 0.0).astype(BF16)
    order = lax.broadcasted_iota(jnp.int32, (tokens, tokens), 0)
    sent = jnp.where(order == route, 1.0, 0.0).astype(BF16)
    pick_out[0] = pick_s
    pick_out[1] = dot(pick_s, sent).astype(BF16)
    place = lax.broadcasted_iota(jnp.int32, (LIVE, tokens), 0)
    live = jnp.where(place == rank, 1.0, 0.0).astype(BF16)
    digits = [d.astype(F32) for d in (ids % 64, ids // 64 % 64, ids // 4096, flags)]
    digits = jnp.concatenate(digits + [jnp.zeros((4, tokens), F32)], axis=0)
    digits = dot(digits.astype(BF16), live, ((1,), (1,))).astype(jnp.int32)
    wanted_out[...] = digits[0:1] + 64 * digits[1:2] + 4096 * digits[2:3]
    mark_out[...] = digits[3:4]


def pick_kernel(near, pick, out):
    rows = near[...].reshape(near.shape[0] * near.shape[1], near.shape[2])
    block = jnp.concatenate([dot(pick[1], rows[:, :QT]), dot(pick[0], rows[:, QT:])], axis=1)
    block = block.astype(BF16)
    for i in range(out.shape[0]):
        out[i] = block


def spread_kernel(gathered, out):
    nz = gathered.shape[0]
    teacher = [gathered[z, :, :QT] for z in range(nz)]
    student = [gathered[z, :, QT:] for z in range(nz)]
    whole = jnp.concatenate(teacher + student, axis=1)
    for i in range(out.shape[0]):
        out[i] = whole


def logits_of(rows, head_s, head_t, core):
    dt = head_t.shape[1]
    s = sum(dot(rows[i, :, dt:], head_s[2 * core + i]) for i in range(2))
    u = sum(dot(rows[i, :, :dt], head_t[2 * core + i]) for i in range(2))
    return s, u


def half_kernel(where, rows, head_s, head_t, s_out, u_out, turned):
    s_out[...], u_out[...] = logits_of(rows, head_s, head_t, where[0])
    for i in range(2):
        turned[i] = rows[i, :, head_t.shape[1] :].T


def stats_kernel(
    where, rows, head_s, head_t, s_own, u_own, wanted, s_t_out, u_t_out, stats_out
):
    core, first_col = where[0], where[1]
    s, u = logits_of(rows, head_s, head_t, 1 - core)
    s_t = (s_own[...] + s).T
    u_t = (u_own[...] + u).T
    s_t_out[...] = s_t
    u_t_out[...] = u_t
    m_s = jnp.max(s_t, axis=0, keepdims=True)
    m_u = jnp.max(u_t, axis=0, keepdims=True)
    s_rel = s_t - m_s
    u_rel = u_t - m_u
    e_s = jnp.exp(s_rel)
    sum_s = jnp.sum(e_s, axis=0, keepdims=True)
    sum_u = jnp.sum(jnp.exp(u_rel), axis=0, keepdims=True)
    mean = jnp.sum(e_s * (s_rel - u_rel), axis=0, keepdims=True) / sum_s
    log_s = jnp.log(sum_s)
    log_u = jnp.log(sum_u)
    column = lax.broadcasted_iota(jnp.int32, s_t.shape, 0)
    hit = column == wanted[...] - first_col
    apart = jnp.sum(jnp.where(hit, u_t - s_t, 0.0), axis=0, keepdims=True)
    block = jnp.concatenate([m_s + log_s, m_u + log_u, mean - log_s + log_u, apart], axis=1)
    for i in range(stats_out.shape[0]):
        stats_out[i] = block


def merge(parts):
    parts = parts[:, 0, :]
    lse_s, lse_u, kl, apart = [parts[:, LIVE * k : LIVE * k + LIVE] for k in range(4)]
    m_s = jnp.max(lse_s, axis=0, keepdims=True)
    m_u = jnp.max(lse_u, axis=0, keepdims=True)
    all_s = m_s + jnp.log(jnp.sum(jnp.exp(lse_s - m_s), axis=0, keepdims=True))
    all_u = m_u + jnp.log(jnp.sum(jnp.exp(lse_u - m_u), axis=0, keepdims=True))
    share = jnp.exp(lse_s - all_s)
    whole = share * (kl + (lse_s - all_s) - (lse_u - all_u))
    whole = jnp.sum(whole, axis=0, keepdims=True)
    return all_s, all_u, whole, jnp.sum(apart, axis=0, keepdims=True)


def merge_kernel(parts, out):
    block = jnp.concatenate(merge(parts[...]), axis=1)
    for i in range(out.shape[0]):
        out[i] = block


def grad_kernel(
    table, parts, s_t, u_t, mark, turned, other, kl_out, grad_out
):
    core, group = table[0], table[2]
    nz = grad_out.shape[0]
    dt = other.shape[2] - nz * QS
    lse_s, lse_u, kl, apart = merge(parts[...])
    mixed = 1.0 / (0.2 * jnp.exp(apart - lse_u + lse_s) + 0.8)
    weight = jnp.where(mark[...] == 1, mixed, jnp.ones_like(mixed))
    log_s = s_t[...] - lse_s
    gap = log_s - (u_t[...] - lse_u)
    d = (weight * jnp.exp(log_s) * (gap - kl)).T.astype(BF16)
    for n in range(4):
        if n < 2:
            block = dot(turned[n], d)
        else:
            block = dot(other[n - 2, :, dt:], d, ((0,), (0,)))
        half = core if n < 2 else 1 - core
        for z in range(nz):
            grad_out[z, 2 * half + n % 2] = block[QS * z : QS * z + QS].astype(BF16)
    start = jnp.int32(0)
    for w in range(table.shape[0] - 5):
        start = start + jnp.where(w < group, table[5 + w], 0)
    row = lax.broadcasted_iota(jnp.int32, (16, LIVE), 0)
    column = lax.broadcasted_iota(jnp.int32, (16, LIVE), 1)
    mine = jnp.logical_and(column == row + start, row < table[5 + group])
    mine = jnp.sum(jnp.where(mine, kl, 0.0), axis=1, keepdims=True)
    kl_out[...] = jnp.broadcast_to(mine, (16, 128)).T[0:1]


def on_device(
    student_hidden, teacher_rows, student_head, teacher_head, lengths, route, sampled_ids, mix_flags
):
    nz = lax.axis_size("z")
    core = lax.axis_index("c")
    x_hi, x_lo = lax.axis_index("xh"), lax.axis_index("xl")
    group = ((lax.axis_index("y") * 2 + x_hi) * 2 + x_lo) * 2 + core
    grp_rows = student_hidden.shape[0]
    ds, vocab_dev = student_head.shape
    dt = teacher_head.shape[0]
    quarter = (ds + dt) // 4
    first_col = (group * nz + lax.axis_index("z")) * vocab_dev
    place = jnp.stack([core, first_col, group, lax.axis_index("y") * 2 + x_hi, x_lo])
    table = jnp.concatenate([place.astype(jnp.int32), lengths])
    rows = jnp.stack([route, sampled_ids, mix_flags])
    tok = ("y", "xh", "xl", "c")

    quarters = pl.pallas_call(
        quarter_kernel,
        out_shape=jax.ShapeDtypeStruct((32, grp_rows, QT + QS), BF16),
        in_specs=[VMEM], out_specs=VMEM,
        compiler_params=pltpu.CompilerParams(
            vmem_limit_bytes=4 * 1024 * 1024, allow_input_fusion=[True]
        ),
    )(jnp.concatenate([teacher_rows, student_hidden], axis=1))
    near = lax.all_to_all(quarters, tok, 0, 0)
    per_row = jax.ShapeDtypeStruct((1, LIVE), jnp.int32)
    pick, wanted, mark = pl.pallas_call(
        index_kernel,
        out_shape=(jax.ShapeDtypeStruct((2, ROWS, route.shape[0]), BF16), per_row, per_row),
        in_specs=[SMEM, VMEM], out_specs=(VMEM,) * 3, compiler_params=grant(6),
    )(table, rows)
    picked = pl.pallas_call(
        pick_kernel,
        out_shape=jax.ShapeDtypeStruct((nz, ROWS, QT + QS), BF16),
        in_specs=[VMEM] * 2, out_specs=VMEM, compiler_params=grant(4),
    )(near, pick)
    gathered = lax.all_to_all(picked, "z", 0, 0)
    copies = pl.pallas_call(
        spread_kernel,
        out_shape=jax.ShapeDtypeStruct((16, ROWS, quarter), BF16),
        in_specs=[VMEM], out_specs=VMEM, compiler_params=grant(8),
    )(gathered)
    own = lax.all_to_all(copies, ("xl", "y", "xh"), 0, 0).reshape(2, LIVE, quarter)
    other = lax.ppermute(own, "c", [(0, 1), (1, 0)])
    head_s = student_head.reshape(nz, 4, QS, vocab_dev).transpose(1, 0, 2, 3)
    head_s = head_s.reshape(4, ds // 4, vocab_dev)
    head_t = teacher_head.reshape(nz, 4, QT, vocab_dev).transpose(1, 0, 2, 3)
    head_t = head_t.reshape(4, dt // 4, vocab_dev)
    logits = jax.ShapeDtypeStruct((LIVE, vocab_dev), F32)
    turned = jax.ShapeDtypeStruct((2, ds // 4, LIVE), BF16)
    s_own, u_own, turned = pl.pallas_call(
        half_kernel, out_shape=(logits, logits, turned),
        in_specs=[SMEM] + [VMEM] * 3, out_specs=(VMEM,) * 3, compiler_params=grant(8),
    )(table, own, head_s, head_t)
    whole = jax.ShapeDtypeStruct((vocab_dev, LIVE), F32)
    s_t, u_t, stats = pl.pallas_call(
        stats_kernel,
        out_shape=(whole, whole, jax.ShapeDtypeStruct((32, 1, 4 * LIVE), F32)),
        in_specs=[SMEM] + [VMEM] * 6, out_specs=(VMEM,) * 3, compiler_params=grant(8),
    )(table, other, head_s, head_t, s_own, u_own, wanted)
    parts = lax.all_to_all(stats, tok, 0, 0)
    merged = pl.pallas_call(
        merge_kernel,
        out_shape=jax.ShapeDtypeStruct((nz, 1, 4 * LIVE), F32),
        in_specs=[VMEM], out_specs=VMEM, compiler_params=grant(4),
    )(parts)
    parts = lax.all_to_all(merged, "z", 0, 0)
    kl_rows, head_grad = pl.pallas_call(
        grad_kernel,
        out_shape=(
            jax.ShapeDtypeStruct((1, grp_rows), F32),
            jax.ShapeDtypeStruct((nz, 4, QS, vocab_dev), BF16),
        ),
        in_specs=[SMEM] + [VMEM] * 6,
        out_specs=(VMEM,) * 2,
        compiler_params=grant(8),
    )(table, parts, s_t, u_t, mark, turned, other)
    return kl_rows[0], head_grad.reshape(ds, vocab_dev)


def solution(mesh):
    axes = ("y", "xh", "xl", "c", "z")
    fine = Mesh(mesh.devices.reshape(4, 2, 2, 2, 16), axes)
    tok = axes[:4]
    in_specs = (P(tok, "z"), P(tok, "z"), P(None, axes), P(None, axes), P(), P(), P(), P())
    out_specs = (P(tok), P(None, axes))
    return jax.shard_map(
        on_device, mesh=fine, in_specs=in_specs, out_specs=out_specs, check_vma=False
    )
```

```python
import jax
import jax.numpy as jnp
from jax import lax
from jax.experimental import pallas as pl
from jax.experimental.pallas import tpu as pltpu
from jax.sharding import Mesh, PartitionSpec as P

F32 = jnp.float32
BF16 = jnp.bfloat16
VMEM = pl.BlockSpec(memory_space=pltpu.VMEM)
SMEM = pl.BlockSpec(memory_space=pltpu.SMEM)
LIVE = 320
ROWS = 40
QT, QS = 64, 40


def grant(mib):
    return pltpu.CompilerParams(vmem_limit_bytes=mib * 1024 * 1024)


def dot(a, b, dims=((1,), (0,))):
    return lax.dot_general(a, b, (dims, ((), ())), preferred_element_type=F32)


def ranks(table, tokens):
    slot = lax.broadcasted_iota(jnp.int32, (1, tokens), 1)
    window, row = slot // 16, slot % 16
    rank = jnp.full((1, tokens), -1, jnp.int32)
    start = jnp.int32(0)
    for w in range(table.shape[0] - 5):
        here = jnp.logical_and(window == w, row < table[5 + w])
        rank = jnp.where(here, row + start, rank)
        start = start + table[5 + w]
    return rank


def quarter_kernel(local, out):
    teacher, student = local[:, : 4 * QT], local[:, 4 * QT :]
    blocks = []
    for q in range(4):
        part = [teacher[:, QT * q : QT * q + QT], student[:, QS * q : QS * q + QS]]
        blocks.append(jnp.concatenate(part, axis=1))
    for i in range(out.shape[0]):
        out[i] = blocks[2 * (i % 2) + i // 2 % 2]


def index_kernel(table, rows, pick_out, wanted_out, mark_out):
    chunk = table[3]
    tokens = rows.shape[1]
    rank = ranks(table, tokens)
    route, ids, flags = rows[0:1], rows[1:2], rows[2:3]
    place = lax.broadcasted_iota(jnp.int32, (ROWS, tokens), 0) + chunk * ROWS
    pick_s = jnp.where(place == rank, 1.0, 0.0).astype(BF16)
    order = lax.broadcasted_iota(jnp.int32, (tokens, tokens), 0)
    sent = jnp.where(order == route, 1.0, 0.0).astype(BF16)
    pick_out[0] = pick_s
    pick_out[1] = dot(pick_s, sent).astype(BF16)
    place = lax.broadcasted_iota(jnp.int32, (LIVE, tokens), 0)
    live = jnp.where(place == rank, 1.0, 0.0).astype(BF16)
    digits = [d.astype(F32) for d in (ids % 64, ids // 64 % 64, ids // 4096, flags)]
    digits = jnp.concatenate(digits + [jnp.zeros((4, tokens), F32)], axis=0)
    digits = dot(digits.astype(BF16), live, ((1,), (1,))).astype(jnp.int32)
    wanted_out[...] = digits[0:1] + 64 * digits[1:2] + 4096 * digits[2:3]
    mark_out[...] = digits[3:4]


def pick_kernel(near, pick, out):
    rows = near[...].reshape(near.shape[0] * near.shape[1], near.shape[2])
    block = jnp.concatenate([dot(pick[1], rows[:, :QT]), dot(pick[0], rows[:, QT:])], axis=1)
    block = block.astype(BF16)
    for i in range(out.shape[0]):
        out[i] = block


def spread_kernel(gathered, out):
    nz = gathered.shape[0]
    teacher = [gathered[z, :, :QT] for z in range(nz)]
    student = [gathered[z, :, QT:] for z in range(nz)]
    whole = jnp.concatenate(teacher + student, axis=1)
    for i in range(out.shape[0]):
        out[i] = whole


def logits_of(rows, head_s, head_t, core):
    dt = head_t.shape[1]
    s = sum(dot(rows[i, :, dt:], head_s[2 * core + i]) for i in range(2))
    u = sum(dot(rows[i, :, :dt], head_t[2 * core + i]) for i in range(2))
    return s, u


def half_kernel(where, rows, head_s, head_t, s_out, u_out, turned):
    s_out[...], u_out[...] = logits_of(rows, head_s, head_t, where[0])
    for i in range(2):
        turned[i] = rows[i, :, head_t.shape[1] :].T


def stats_kernel(
    where, rows, head_s, head_t, s_own, u_own, wanted, s_t_out, u_t_out, stats_out
):
    core, first_col = where[0], where[1]
    s, u = logits_of(rows, head_s, head_t, 1 - core)
    s_t = (s_own[...] + s).T
    u_t = (u_own[...] + u).T
    s_t_out[...] = s_t
    u_t_out[...] = u_t
    m_s = jnp.max(s_t, axis=0, keepdims=True)
    m_u = jnp.max(u_t, axis=0, keepdims=True)
    s_rel = s_t - m_s
    u_rel = u_t - m_u
    e_s = jnp.exp(s_rel)
    sum_s = jnp.sum(e_s, axis=0, keepdims=True)
    sum_u = jnp.sum(jnp.exp(u_rel), axis=0, keepdims=True)
    mean = jnp.sum(e_s * (s_rel - u_rel), axis=0, keepdims=True) / sum_s
    log_s = jnp.log(sum_s)
    log_u = jnp.log(sum_u)
    column = lax.broadcasted_iota(jnp.int32, s_t.shape, 0)
    hit = column == wanted[...] - first_col
    apart = jnp.sum(jnp.where(hit, u_t - s_t, 0.0), axis=0, keepdims=True)
    block = jnp.concatenate([m_s + log_s, m_u + log_u, mean - log_s + log_u, apart], axis=1)
    for i in range(stats_out.shape[0]):
        stats_out[i] = block


def merge(parts):
    parts = parts[:, 0, :]
    lse_s, lse_u, kl, apart = [parts[:, LIVE * k : LIVE * k + LIVE] for k in range(4)]
    m_s = jnp.max(lse_s, axis=0, keepdims=True)
    m_u = jnp.max(lse_u, axis=0, keepdims=True)
    all_s = m_s + jnp.log(jnp.sum(jnp.exp(lse_s - m_s), axis=0, keepdims=True))
    all_u = m_u + jnp.log(jnp.sum(jnp.exp(lse_u - m_u), axis=0, keepdims=True))
    share = jnp.exp(lse_s - all_s)
    whole = share * (kl + (lse_s - all_s) - (lse_u - all_u))
    whole = jnp.sum(whole, axis=0, keepdims=True)
    return all_s, all_u, whole, jnp.sum(apart, axis=0, keepdims=True)


def merge_kernel(parts, out):
    block = jnp.concatenate(merge(parts[...]), axis=1)
    for i in range(out.shape[0]):
        out[i] = block


def grad_kernel(
    table, parts, s_t, u_t, mark, turned, other, kl_out, grad_out, ready, sent
):
    core, group = table[0], table[2]
    nz = grad_out.shape[0]
    dt = other.shape[2] - nz * QS
    lse_s, lse_u, kl, apart = merge(parts[...])
    mixed = 1.0 / (0.2 * jnp.exp(apart - lse_u + lse_s) + 0.8)
    weight = jnp.where(mark[...] == 1, mixed, jnp.ones_like(mixed))
    log_s = s_t[...] - lse_s
    gap = log_s - (u_t[...] - lse_u)
    d_t = (weight * jnp.exp(log_s) * (gap - kl)).astype(BF16)
    leaving = []
    for n in range(4):
        if n < 2:
            block = dot(turned[n], d_t, ((1,), (1,)))
        else:
            block = dot(d_t, other[n - 2, :, dt:]).T
        for z in range(nz):
            ready[n, z] = block[QS * z : QS * z + QS].astype(BF16)
        half = core if n < 2 else 1 - core
        copy = pltpu.make_async_copy(ready.at[n], grad_out.at[:, 2 * half + n % 2], sent.at[n])
        copy.start()
        leaving.append(copy)
    start = jnp.int32(0)
    for w in range(table.shape[0] - 5):
        start = start + jnp.where(w < group, table[5 + w], 0)
    row = lax.broadcasted_iota(jnp.int32, (16, LIVE), 0)
    column = lax.broadcasted_iota(jnp.int32, (16, LIVE), 1)
    mine = jnp.logical_and(column == row + start, row < table[5 + group])
    mine = jnp.sum(jnp.where(mine, kl, 0.0), axis=1, keepdims=True)
    kl_out[...] = jnp.broadcast_to(mine, (16, 128)).T[0:1]
    for copy in leaving:
        copy.wait()


def on_device(
    student_hidden, teacher_rows, student_head, teacher_head, lengths, route, sampled_ids, mix_flags
):
    nz = lax.axis_size("z")
    core = lax.axis_index("c")
    x_hi, x_lo = lax.axis_index("xh"), lax.axis_index("xl")
    group = ((lax.axis_index("y") * 2 + x_hi) * 2 + x_lo) * 2 + core
    grp_rows = student_hidden.shape[0]
    ds, vocab_dev = student_head.shape
    dt = teacher_head.shape[0]
    quarter = (ds + dt) // 4
    first_col = (group * nz + lax.axis_index("z")) * vocab_dev
    place = jnp.stack([core, first_col, group, lax.axis_index("y") * 2 + x_hi, x_lo])
    table = jnp.concatenate([place.astype(jnp.int32), lengths])
    rows = jnp.stack([route, sampled_ids, mix_flags])
    tok = ("y", "xh", "xl", "c")

    quarters = pl.pallas_call(
        quarter_kernel,
        out_shape=jax.ShapeDtypeStruct((32, grp_rows, QT + QS), BF16),
        in_specs=[VMEM], out_specs=VMEM,
        compiler_params=pltpu.CompilerParams(
            vmem_limit_bytes=4 * 1024 * 1024, allow_input_fusion=[True]
        ),
    )(jnp.concatenate([teacher_rows, student_hidden], axis=1))
    near = lax.all_to_all(quarters, tok, 0, 0)
    per_row = jax.ShapeDtypeStruct((1, LIVE), jnp.int32)
    pick, wanted, mark = pl.pallas_call(
        index_kernel,
        out_shape=(jax.ShapeDtypeStruct((2, ROWS, route.shape[0]), BF16), per_row, per_row),
        in_specs=[SMEM, VMEM], out_specs=(VMEM,) * 3, compiler_params=grant(6),
    )(table, rows)
    picked = pl.pallas_call(
        pick_kernel,
        out_shape=jax.ShapeDtypeStruct((nz, ROWS, QT + QS), BF16),
        in_specs=[VMEM] * 2, out_specs=VMEM, compiler_params=grant(4),
    )(near, pick)
    gathered = lax.all_to_all(picked, "z", 0, 0)
    copies = pl.pallas_call(
        spread_kernel,
        out_shape=jax.ShapeDtypeStruct((16, ROWS, quarter), BF16),
        in_specs=[VMEM], out_specs=VMEM, compiler_params=grant(8),
    )(gathered)
    own = lax.all_to_all(copies, ("xl", "y", "xh"), 0, 0).reshape(2, LIVE, quarter)
    other = lax.ppermute(own, "c", [(0, 1), (1, 0)])
    head_s = student_head.reshape(nz, 4, QS, vocab_dev).transpose(1, 0, 2, 3)
    head_s = head_s.reshape(4, ds // 4, vocab_dev)
    head_t = teacher_head.reshape(nz, 4, QT, vocab_dev).transpose(1, 0, 2, 3)
    head_t = head_t.reshape(4, dt // 4, vocab_dev)
    logits = jax.ShapeDtypeStruct((LIVE, vocab_dev), F32)
    turned = jax.ShapeDtypeStruct((2, ds // 4, LIVE), BF16)
    s_own, u_own, turned = pl.pallas_call(
        half_kernel, out_shape=(logits, logits, turned),
        in_specs=[SMEM] + [VMEM] * 3, out_specs=(VMEM,) * 3, compiler_params=grant(8),
    )(table, own, head_s, head_t)
    whole = jax.ShapeDtypeStruct((vocab_dev, LIVE), F32)
    s_t, u_t, stats = pl.pallas_call(
        stats_kernel,
        out_shape=(whole, whole, jax.ShapeDtypeStruct((32, 1, 4 * LIVE), F32)),
        in_specs=[SMEM] + [VMEM] * 6, out_specs=(VMEM,) * 3, compiler_params=grant(8),
    )(table, other, head_s, head_t, s_own, u_own, wanted)
    parts = lax.all_to_all(stats, tok, 0, 0)
    merged = pl.pallas_call(
        merge_kernel,
        out_shape=jax.ShapeDtypeStruct((nz, 1, 4 * LIVE), F32),
        in_specs=[VMEM], out_specs=VMEM, compiler_params=grant(4),
    )(parts)
    parts = lax.all_to_all(merged, "z", 0, 0)
    kl_rows, head_grad = pl.pallas_call(
        grad_kernel,
        out_shape=(
            jax.ShapeDtypeStruct((1, grp_rows), F32),
            jax.ShapeDtypeStruct((nz, 4, QS, vocab_dev), BF16),
        ),
        in_specs=[SMEM] + [VMEM] * 6,
        out_specs=(VMEM, pl.BlockSpec(memory_space=pl.ANY)),
        scratch_shapes=[
            pltpu.VMEM((4, nz, QS, vocab_dev), BF16), pltpu.SemaphoreType.DMA((4,))
        ],
        compiler_params=grant(8),
    )(table, parts, s_t, u_t, mark, turned, other)
    return kl_rows[0], head_grad.reshape(ds, vocab_dev)


def solution(mesh):
    axes = ("y", "xh", "xl", "c", "z")
    fine = Mesh(mesh.devices.reshape(4, 2, 2, 2, 16), axes)
    tok = axes[:4]
    in_specs = (P(tok, "z"), P(tok, "z"), P(None, axes), P(None, axes), P(), P(), P(), P())
    out_specs = (P(tok), P(None, axes))
    return jax.shard_map(
        on_device, mesh=fine, in_specs=in_specs, out_specs=out_specs, check_vma=False
    )
```
